32 devices in a mesh: image: 8 (over z, core), band: 4 (over y, x).
Axes of the slice: x: 2, y: 2, z: 4, core: 2. Of those that a mesh axis runs over, the one named last changes fastest.
Arguments:
- images: float32 [8, 128, 16, 128], P('image', None, 'band'), may hold values from -60 to 60, as said below
- cotangent: float32 [8, 128, 16, 128], P('image', None, 'band'), may hold values from -6 to 6
- filters: float32 [2, 1152, 128], replicated, may hold values from -6 to 6
- rates: float32 [2], replicated, may hold values from 0.002 to 0.008
Outputs:
- new_filters: float32 [8, 2, 1152, 128], P('image')
The draws below stay inside these ranges and needn't reach their ends.
Inputs may be any that keep to these rules, and one draw needn't show every extreme that they name: `images`: Real-valued feature maps whose channels differ in scale.
All inputs are finite; a program needn't handle non-finite values.
Results may differ from the reference program's by a relative error of at most 0.0001.
Values sent between devices are 32-bit elements; how exact they have to be, the bound alone decides.
No kernel may reach another device: no remote copies, remote signals or barrier semaphores. Data moves between devices by JAX's collectives and lax.ppermute only.
A program may use at most 64 MiB of HBM per device.

```python
import math
import jax
import jax.numpy as jnp
from jax import lax

C = 128
COLS = 128
IMAGES = 8
HEIGHT = 16
N_IMAGE = 8


def draw_images(key, part):
    key_scale = jax.random.fold_in(key, 11)
    key_value = jax.random.fold_in(key, 23)
    levels = (jnp.arange(C, dtype=jnp.float32) + jax.random.uniform(key_scale, (C,), jnp.float32)) / C
    channel_scale = 10.0 ** levels
    values = jax.random.normal(key_value, (IMAGES, C, HEIGHT, COLS), jnp.float32)
    return jnp.clip(values * channel_scale[None, :, None, None], -60.0, 60.0)


def block_levels(key, extent, cuts, least, high):
    def one(axis_at, parts):
        steps = jax.random.uniform(jax.random.fold_in(jax.random.fold_in(key, 6), axis_at), (parts,), jnp.float32, least / len(cuts), high / len(cuts))
        return jnp.repeat(jnp.exp(steps), extent[axis_at] // parts).reshape((-1,) + (1,) * (len(extent) - axis_at - 1))

    level = one(*cuts[0])
    for cut in cuts[1:]:
        level = level * one(*cut)
    return level


def gaussian(key, extent, spread, bound, cuts=(), held_as=jnp.bfloat16):
    drawn = spread * jax.random.normal(key, extent, jnp.float32)
    if cuts:
        drawn = drawn * block_levels(key, extent, cuts, -0.22, 0.18)
    return jnp.clip(drawn, -bound, bound).astype(held_as)


def setup_inputs(seed: int = 0) -> dict:
    keys = jax.random.split(jax.random.key(seed), 5)
    images = draw_images(jax.random.fold_in(keys[4], 71), 0)
    cotangent = gaussian(keys[1], (IMAGES, C, HEIGHT, COLS), 1.0, 6.0, ((0, 8), (2, 4)), jnp.float32)
    filters = gaussian(keys[2], (2, 9 * C, C), 1.0, 6.0, (), jnp.float32)
    rates = jnp.clip(jnp.exp(jax.random.uniform(keys[3], (2,), jnp.float32, math.log(0.002), math.log(0.008))), 0.002, 0.008)
    return {"images": images, "cotangent": cotangent, "filters": filters, "rates": rates}


HIGH = lax.Precision.HIGHEST


def taps(padded, rows, cols):
    chans = padded.shape[0]
    pieces = [padded[:, dr:dr + rows, dc:dc + cols] for dr in range(3) for dc in range(3)]
    return jnp.stack(pieces, axis=1).reshape(chans * 9, rows * cols)


def flipped(padded, rows, cols):
    chans = padded.shape[0]
    pieces = [padded[:, 2 - dr:2 - dr + rows, 2 - dc:2 - dc + cols] for dr in range(3) for dc in range(3)]
    return jnp.stack(pieces, axis=1).reshape(chans, 9, rows * cols)


def reference(images, cotangent, filters, rates):
    chans = images.shape[1]
    height = images.shape[2]
    cols = images.shape[3]
    scale = (9 * chans) ** -0.5

    def image_grads(pair):
        feats, cot = pair
        first = jnp.pad(feats, ((0, 0), (1, 1), (1, 1)))
        patch_one = taps(first, height, cols)
        pre = scale * jnp.einsum("kc,kp->cp", filters[0], patch_one, precision=HIGH)
        hidden = jax.nn.silu(pre).reshape(chans, height, cols)
        patch_two = taps(jnp.pad(hidden, ((0, 0), (1, 1), (1, 1))), height, cols)
        flat_cot = cot.reshape(chans, height * cols)
        grad_two = scale * jnp.einsum("kp,cp->kc", patch_two, flat_cot, precision=HIGH)
        back = flipped(jnp.pad(cot, ((0, 0), (1, 1), (1, 1))), height, cols)
        weight_two = filters[1].reshape(chans, 9, chans)
        dhidden = scale * jnp.einsum("itc,ctp->ip", weight_two, back, precision=HIGH)
        sig = jax.nn.sigmoid(pre)
        dpre = dhidden * sig * (1.0 + pre * (1.0 - sig))
        grad_one = scale * jnp.einsum("kp,cp->kc", patch_one, dpre, precision=HIGH)
        return jnp.stack([grad_one, grad_two])

    grads = lax.map(image_grads, (images, cotangent))
    count = N_IMAGE
    kdim = grads.shape[2]
    levels = count.bit_length() - 1
    for level in range(levels):
        stride = 2 ** level
        view = grads.reshape(count // (2 * stride), 2, stride, 2, kdim, chans)
        lower = view[:, 0]
        upper = view[:, 1]
        inner = jnp.sum(lower * upper, axis=(-2, -1))
        lower_sq = jnp.sum(lower * lower, axis=(-2, -1))
        upper_sq = jnp.sum(upper * upper, axis=(-2, -1))
        coef_low = (1.0 - inner / (2.0 * (lower_sq + 1e-6)))[..., None, None]
        coef_up = (1.0 - inner / (2.0 * (upper_sq + 1e-6)))[..., None, None]
        merged = coef_low * lower + coef_up * upper
        grads = jnp.stack([merged, merged], axis=1).reshape(count, 2, kdim, chans)
    return filters[None] - rates[None, :, None, None] * grads
```

```python
import functools

import jax
import jax.numpy as jnp
from jax import lax
from jax.experimental import pallas as pl
from jax.experimental.pallas import tpu as pltpu
from jax.sharding import PartitionSpec as P

HIGH = lax.Precision.HIGHEST
F32 = jnp.float32
BF16 = jnp.bfloat16


def call(body, outs, scratch=(), flops=0, nbytes=0):
    return pl.pallas_call(
        body,
        out_shape=[jax.ShapeDtypeStruct(s, F32) for s in outs],
        scratch_shapes=list(scratch),
        cost_estimate=pl.CostEstimate(
            flops=flops, bytes_accessed=nbytes, transcendentals=0
        ),
        compiler_params=pltpu.CompilerParams(vmem_limit_bytes=48 * 2**20),
    )


def edges_kernel(rows, x_ref, c_ref, down_ref, up_ref):
    chans = x_ref.shape[0] // rows
    for slot, ref in enumerate((x_ref, c_ref)):
        at = slice(slot * chans, (slot + 1) * chans)
        up_ref[at, :] = ref[pl.ds(0, chans, stride=rows), :]
        down_ref[at, :] = ref[pl.ds(rows - 1, chans, stride=rows), :]


def halves(value):
    high = value.astype(BF16)
    return high, (value - high.astype(F32)).astype(BF16)


def dot3(ah, al, bh, bl, dims):
    def one(a, b):
        return lax.dot_general(a, b, (dims, ((), ())), preferred_element_type=F32)

    return one(ah, bh) + (one(ah, bl) + one(al, bh))


def moved(value, step):
    cols = value.shape[-1]
    col = lax.broadcasted_iota(jnp.int32, value.shape, value.ndim - 1)
    if step > 0:
        return jnp.where(col == cols - 1, 0.0, pltpu.roll(value, cols - 1, 1))
    return jnp.where(col == 0, 0.0, pltpu.roll(value, 1, 1))


def grads_kernel(
    rows, scale, n_band, x_ref, c_ref, prev_ref, next_ref, f_ref, *rest
):
    outs = rest[:n_band]
    g_ref, xh, xl, ch, cl, fh, fl, dh, dl = rest[n_band:]
    chans = x_ref.shape[0] // rows
    cols = x_ref.shape[1]

    def row_of(ref, slot, row):
        if row < 0:
            return prev_ref[slot * chans : (slot + 1) * chans, :]
        if row == rows:
            return next_ref[slot * chans : (slot + 1) * chans, :]
        return ref[pl.ds(row, chans, stride=rows), :]

    def put(high_ref, low_ref, at, row, value):
        high, low = halves(value)
        part = (slice(at * chans, (at + 1) * chans), slice(row * cols, (row + 1) * cols))
        high_ref[part] = high
        low_ref[part] = low

    for row in range(-1, rows + 1):
        value = row_of(x_ref, 0, row)
        other = row_of(c_ref, 1, row)
        for a in range(3):
            if 0 <= row - a + 1 < rows:
                put(xh, xl, a, row - a + 1, value)
            if 0 <= row + a - 1 < rows:
                put(ch, cl, a, row + a - 1, other)
    for a in range(3):
        for b in range(3):
            tap = f_ref[0, pl.ds(3 * a + b, chans, stride=9), :]
            put(fh, fl, b, a, tap.T)
    pre3 = dot3(fh[...], fl[...], xh[...], xl[...], ((1,), (0,)))
    for a in range(3):
        for b in range(3):
            put(fh, fl, b, a, f_ref[1, pl.ds(3 * a + b, chans, stride=9), :])
    back3 = dot3(fh[...], fl[...], ch[...], cl[...], ((1,), (0,)))
    dpres = []
    for row in range(rows):
        at = slice(row * cols, (row + 1) * cols)
        pre = scale * (
            pre3[chans : 2 * chans, at]
            + moved(pre3[:chans, at], -1)
            + moved(pre3[2 * chans :, at], 1)
        )
        dhidden = scale * (
            back3[chans : 2 * chans, at]
            + moved(back3[:chans, at], 1)
            + moved(back3[2 * chans :, at], -1)
        )
        sig = jax.nn.sigmoid(pre)
        hidden = pre * sig
        dpre = dhidden * sig * (1.0 + pre * (1.0 - sig))
        dpres.append(dpre)
        for b, value in enumerate((moved(hidden, -1), hidden, moved(hidden, 1))):
            put(dh, dl, b, row, value)
    grad2 = dot3(dh[...], dl[...], ch[...], cl[...], ((1,), (1,)))
    for a in range(3):
        for b in range(3):
            t = 3 * a + b
            g_ref[1, t * chans : (t + 1) * chans, :] = (
                scale * grad2[b * chans : (b + 1) * chans, a * chans : (a + 1) * chans]
            )
    for row, dpre in enumerate(dpres):
        for b, value in enumerate((moved(dpre, 1), dpre, moved(dpre, -1))):
            put(dh, dl, b, row, value)
    grad1 = dot3(xh[...], xl[...], dh[...], dl[...], ((1,), (1,)))
    for a in range(3):
        for b in range(3):
            t = 3 * a + b
            g_ref[0, t * chans : (t + 1) * chans, :] = (
                scale * grad1[a * chans : (a + 1) * chans, b * chans : (b + 1) * chans]
            )
    band = lax.axis_index("band")
    size = g_ref.shape[1] // n_band
    for k, out in enumerate(outs):
        start = pl.multiple_of(lax.bitwise_xor(band, k) * size, 8)
        for layer in range(2):
            out[layer] = g_ref[layer, pl.ds(start, size), :]


def sum_kernel(n_band, *refs):
    parts, (keep_ref, give_ref) = refs[:n_band], refs[n_band:]
    mine = lax.axis_index("image") % 2
    for out, layer in ((keep_ref, mine), (give_ref, 1 - mine)):
        total = parts[0][layer]
        for part in parts[1:]:
            total = total + part[layer]
        out[...] = total


def pack_kernel(n_pair, keep_ref, other_ref, *outs):
    image = lax.axis_index("image")
    mine = image % 2
    pair = image // 2
    size = keep_ref.shape[0] // n_pair
    for k, out in enumerate(outs):
        start = pl.multiple_of(lax.bitwise_xor(pair, k) * size, 8)
        out[mine] = keep_ref[pl.ds(start, size), :]
        out[1 - mine] = other_ref[pl.ds(start, size), :]


def gram_kernel(n_pair, *refs):
    parts, out = refs[:n_pair], refs[n_pair]
    held = refs[n_pair + 1]
    pair = lax.axis_index("image") // 2
    for k, part in enumerate(parts):
        at = lax.bitwise_xor(pair, k) * 2
        held[at] = part[0]
        held[at + 1] = part[1]
    count = 2 * n_pair
    row = lax.broadcasted_iota(jnp.int32, out.shape, 0)
    col = lax.broadcasted_iota(jnp.int32, out.shape, 1)
    total = jnp.zeros(out.shape, F32)
    for i in range(count):
        for j in range(i, count):
            value = jnp.sum(held[i] * held[j], keepdims=True)
            here = ((row == i) & (col == j)) | ((row == j) & (col == i))
            total = jnp.where(here, value, total)
    out[...] = total


def merge_kernel(n_pair, n_band, sums_ref, *refs):
    parts, out = refs[:n_pair], refs[n_pair]
    image = lax.axis_index("image")
    mine = image % 2
    pair = image // 2
    count = 2 * n_pair
    gram = jnp.zeros(sums_ref.shape[1:], F32)
    for half in range(n_pair):
        for at in range(n_band):
            gram = gram + sums_ref[(2 * half + mine) * n_band + at]
    row = lax.broadcasted_iota(jnp.int32, gram.shape, 0)
    col = lax.broadcasted_iota(jnp.int32, gram.shape, 1)

    def swap(value, axis, step):
        size = value.shape[axis]
        index = row if axis == 0 else col
        return jnp.where(
            (index & step) != 0,
            pltpu.roll(value, step, axis),
            pltpu.roll(value, size - step, axis),
        )

    weight = jnp.ones((count, 1), F32)
    step = 1
    while step < count:
        own = jnp.where(row == col, gram, 0.0)
        cross = jnp.where((row ^ step) == col, gram, 0.0)
        down = 1.0 - jnp.sum(cross, 1, keepdims=True) / (
            2.0 * (jnp.sum(own, 1, keepdims=True) + 1e-06)
        )
        along = 1.0 - jnp.sum(cross, 0, keepdims=True) / (
            2.0 * (jnp.sum(own, 0, keepdims=True) + 1e-06)
        )
        weight = weight * down
        gram = gram * down * along
        gram = gram + swap(gram, 0, step)
        gram = gram + swap(gram, 1, step)
        step *= 2
    place = lax.broadcasted_iota(jnp.int32, weight.shape, 0)
    total = jnp.zeros(out.shape, F32)
    for k, part in enumerate(parts):
        at = lax.bitwise_xor(pair, k) * 2
        for j in range(2):
            factor = jnp.sum(jnp.where(place == at + j, weight, 0.0), keepdims=True)
            total = total + factor * part[j]
    out[...] = total


def gather_kernel(n_pair, *refs):
    parts, out = refs[:n_pair], refs[n_pair]
    pair = lax.axis_index("image") // 2
    size = parts[0].shape[0]
    for k, part in enumerate(parts):
        start = pl.multiple_of(lax.bitwise_xor(pair, k) * size, 8)
        out[pl.ds(start, size), :] = part[...]


def final_kernel(n_band, chans, rates_ref, f_ref, *refs):
    own, others = refs[:n_band], refs[n_band : 2 * n_band]
    out = refs[2 * n_band]
    held = refs[2 * n_band + 1]
    mine = lax.axis_index("image") % 2
    band = lax.axis_index("band")
    size = own[0].shape[0]
    for k in range(n_band):
        start = pl.multiple_of(lax.bitwise_xor(band, k) * size, 8)
        held[mine, pl.ds(start, size), :] = own[k][...]
        held[1 - mine, pl.ds(start, size), :] = others[k][...]
    for layer in range(2):
        rate = rates_ref[layer]
        for t in range(9):
            at = pl.ds(t, chans, stride=9)
            out[0, layer, at, :] = (
                f_ref[layer, at, :] - rate * held[layer, t * chans : (t + 1) * chans, :]
            )


def xor_route(count, k):
    return [(i, i ^ k) for i in range(count)]


def fast(images, cotangent, filters, rates):
    _, chans, rows, cols = images.shape
    n_band = lax.axis_size("band")
    n_image = lax.axis_size("image")
    n_pair = n_image // 2
    kdim = filters.shape[1]
    block = kdim // n_band
    slot = block // n_pair
    scale = kdim ** (-0.5)
    x = images.reshape(chans * rows, cols)
    cot = cotangent.reshape(chans * rows, cols)
    down, up = call(functools.partial(edges_kernel, rows), [(2 * chans, cols)] * 2)(x, cot)
    fwd = [(i, i + 1) for i in range(n_band - 1)]
    bwd = [(j, i) for i, j in fwd]
    before = lax.ppermute(down, "band", fwd)
    after = lax.ppermute(up, "band", bwd)
    wide = (3 * chans, rows * cols)
    parts = call(
        functools.partial(grads_kernel, rows, scale, n_band),
        [(2, block, chans)] * n_band,
        [pltpu.VMEM((2, kdim, chans), F32)]
        + [pltpu.VMEM(wide, BF16)] * 4
        + [pltpu.VMEM((3 * chans, 3 * chans), BF16)] * 2
        + [pltpu.VMEM(wide, BF16)] * 2,
        flops=24 * kdim * chans * rows * cols,
        nbytes=4 * (2 * chans * rows * cols + 4 * kdim * chans),
    )(x, cot, before, after, filters)
    parts = [parts[0]] + [
        lax.ppermute(parts[k], "band", xor_route(n_band, k)) for k in range(1, n_band)
    ]
    keep, give = call(functools.partial(sum_kernel, n_band), [(block, chans)] * 2)(*parts)
    other = lax.ppermute(give, "image", xor_route(n_image, 1))
    parts = call(functools.partial(pack_kernel, n_pair), [(2, slot, chans)] * n_pair)(keep, other)
    parts = [parts[0]] + [
        lax.ppermute(parts[k], "image", xor_route(n_image, 2 * k)) for k in range(1, n_pair)
    ]
    (gram,) = call(
        functools.partial(gram_kernel, n_pair),
        [(n_image, 128)],
        [pltpu.VMEM((n_image, slot, chans), F32)],
    )(*parts)
    sums = jnp.broadcast_to(gram[None], (n_image * n_band,) + gram.shape)
    sums = lax.all_to_all(sums, ("image", "band"), 0, 0, tiled=True)
    (mine,) = call(functools.partial(merge_kernel, n_pair, n_band), [(slot, chans)])(sums, *parts)
    pieces = [mine] + [
        lax.ppermute(mine, "image", xor_route(n_image, 2 * k)) for k in range(1, n_pair)
    ]
    (mine,) = call(functools.partial(gather_kernel, n_pair), [(block, chans)])(*pieces)
    own = [mine] + [
        lax.ppermute(mine, "band", xor_route(n_band, k)) for k in range(1, n_band)
    ]
    others = [lax.ppermute(piece, "image", xor_route(n_image, 1)) for piece in own]
    out = pl.pallas_call(
        functools.partial(final_kernel, n_band, chans),
        out_shape=jax.ShapeDtypeStruct((1,) + filters.shape, F32),
        in_specs=[pl.BlockSpec(memory_space=pltpu.SMEM)]
        + [pl.BlockSpec(memory_space=pltpu.VMEM)] * (1 + 2 * n_band),
        scratch_shapes=[pltpu.VMEM(filters.shape, F32)],
        compiler_params=pltpu.CompilerParams(vmem_limit_bytes=48 * 2**20),
    )(rates, filters, *own, *others)
    return out


def with_rims(field):
    count = lax.axis_size("band")
    forward = [(i, i + 1) for i in range(count - 1)]
    backward = [(target, source) for source, target in forward]
    low = lax.ppermute(field[:, -1:], "band", forward)
    high = lax.ppermute(field[:, :1], "band", backward)
    extended = jnp.concatenate([low, field, high], axis=1)
    return jnp.pad(extended, ((0, 0), (0, 0), (1, 1)))


def taps(padded, rows, cols, flip=False):
    chans = padded.shape[0]
    at = (2, 1, 0) if flip else (0, 1, 2)
    pieces = [padded[:, dr : dr + rows, dc : dc + cols] for dr in at for dc in at]
    return jnp.stack(pieces, axis=1).reshape(chans, 9, rows * cols)


def plain(images, cotangent, filters, rates):
    feats, cot = images[0], cotangent[0]
    chans, rows, cols = feats.shape
    scale = (9 * chans) ** (-0.5)
    patch_one = taps(with_rims(feats), rows, cols).reshape(9 * chans, rows * cols)
    pre = scale * jnp.einsum("kc,kp->cp", filters[0], patch_one, precision=HIGH)
    hidden = jax.nn.silu(pre).reshape(chans, rows, cols)
    patch_two = taps(with_rims(hidden), rows, cols).reshape(9 * chans, rows * cols)
    back = taps(with_rims(cot), rows, cols, flip=True)
    flat_cot = cot.reshape(chans, rows * cols)
    grad_two = scale * jnp.einsum("kp,cp->kc", patch_two, flat_cot, precision=HIGH)
    weight_two = filters[1].reshape(chans, 9, chans)
    dhidden = scale * jnp.einsum("itc,ctp->ip", weight_two, back, precision=HIGH)
    sig = jax.nn.sigmoid(pre)
    dpre = dhidden * sig * (1.0 + pre * (1.0 - sig))
    grad_one = scale * jnp.einsum("kp,cp->kc", patch_one, dpre, precision=HIGH)
    block = lax.psum_scatter(
        jnp.stack([grad_one, grad_two]), "band", scatter_dimension=1, tiled=True
    )
    count = lax.axis_size("image")
    for level in range(count.bit_length() - 1):
        other = lax.ppermute(block, "image", xor_route(count, 1 << level))
        inner, own_sq, other_sq = lax.psum(
            tuple(jnp.sum(v, axis=(1, 2)) for v in (block * other, block * block, other * other)),
            "band",
        )
        low = (1.0 - inner / (2.0 * (own_sq + 1e-06)))[:, None, None]
        high = (1.0 - inner / (2.0 * (other_sq + 1e-06)))[:, None, None]
        block = low * block + high * other
    height = block.shape[1]
    mine = lax.dynamic_slice_in_dim(filters, lax.axis_index("band") * height, height, 1)
    fresh = (mine - rates[:, None, None] * block)[None]
    return lax.all_gather(fresh, "band", axis=2, tiled=True)


def local(images, cotangent, filters, rates):
    n_band = lax.axis_size("band")
    n_image = lax.axis_size("image")
    kdim = filters.shape[1]
    fits = (
        n_image >= 4
        and n_image & (n_image - 1) == 0
        and n_band & (n_band - 1) == 0
        and kdim % (n_band * (n_image // 2) * 8) == 0
    )
    return (fast if fits else plain)(images, cotangent, filters, rates)


def solution(mesh):
    in_specs = (P("image", None, "band", None), P("image", None, "band", None), P(), P())
    out_specs = P("image", None, None, None)
    return jax.shard_map(local, mesh=mesh, in_specs=in_specs, out_specs=out_specs, check_vma=False)
```

```python
import functools

import jax
import jax.numpy as jnp
from jax import lax
from jax.experimental import pallas as pl
from jax.experimental.pallas import tpu as pltpu
from jax.sharding import PartitionSpec as P


HIGH = lax.Precision.HIGHEST
F32 = jnp.float32
BF16 = jnp.bfloat16


def call(body, outs, scratch=(), flops=0, nbytes=0):
    return pl.pallas_call(
        body,
        out_shape=[jax.ShapeDtypeStruct(s, F32) for s in outs],
        scratch_shapes=list(scratch),
        cost_estimate=pl.CostEstimate(
            flops=flops, bytes_accessed=nbytes, transcendentals=0
        ),
        compiler_params=pltpu.CompilerParams(vmem_limit_bytes=48 * 2**20),
    )


def edges_kernel(x_hbm, c_hbm, down_ref, up_ref, x_ref, c_ref, sems):
    copies = [
        pltpu.make_async_copy(x_hbm, x_ref, sems.at[0]),
        pltpu.make_async_copy(c_hbm, c_ref, sems.at[1]),
    ]
    for copy in copies:
        copy.start()
    chans = down_ref.shape[0] // 2
    rows = x_ref.shape[0] // chans
    for slot, ref in enumerate((x_ref, c_ref)):
        copies[slot].wait()
        at = slice(slot * chans, (slot + 1) * chans)
        up_ref[at, :] = ref[pl.ds(0, chans, stride=rows), :]
        down_ref[at, :] = ref[pl.ds(rows - 1, chans, stride=rows), :]


def halves(value):
    high = value.astype(BF16)
    return high, (value - high.astype(F32)).astype(BF16)


def dot3(ah, al, bh, bl, dims):
    def one(a, b):
        return lax.dot_general(a, b, (dims, ((), ())), preferred_element_type=F32)

    return one(ah, bh) + (one(ah, bl) + one(al, bh))


def moved(value, step):
    cols = value.shape[-1]
    col = lax.broadcasted_iota(jnp.int32, value.shape, value.ndim - 1)
    if step > 0:
        return jnp.where(col == cols - 1, 0.0, pltpu.roll(value, cols - 1, 1))
    return jnp.where(col == 0, 0.0, pltpu.roll(value, 1, 1))


def put(high_ref, low_ref, at, row, value):
    high, low = halves(value)
    rows, cols = value.shape
    part = (slice(at * rows, (at + 1) * rows), slice(row * cols, (row + 1) * cols))
    high_ref[part] = high
    low_ref[part] = low


def inner_kernel(rows, x_ref, c_ref, f_ref, *refs):
    xh, xl, ch, cl, fh, fl, gh, gl, pre_ref, back_ref = refs
    chans = x_ref.shape[0] // rows
    cols = x_ref.shape[1]
    blank = jnp.zeros((chans, cols), F32)
    for row in range(-1, rows + 1):
        inside = 0 <= row < rows
        at = pl.ds(row, chans, stride=rows)
        value = x_ref[at, :] if inside else blank
        other = c_ref[at, :] if inside else blank
        for a in range(3):
            if 0 <= row - a + 1 < rows:
                put(xh, xl, a, row - a + 1, value)
            if 0 <= row + a - 1 < rows:
                put(ch, cl, a, row + a - 1, other)
    for a in range(3):
        for b in range(3):
            at = pl.ds(3 * a + b, chans, stride=9)
            put(fh, fl, b, a, f_ref[0, at, :].T)
            put(gh, gl, b, a, f_ref[1, at, :])
    pre_ref[...] = dot3(fh[...], fl[...], xh[...], xl[...], ((1,), (0,)))
    back_ref[...] = dot3(gh[...], gl[...], ch[...], cl[...], ((1,), (0,)))


def grads_kernel(rows, scale, n_band, cuts, *refs):
    prev_ref, next_ref, xh, xl, ch, cl, fh, fl, gh, gl, pre_ref, back_ref = refs[:12]
    outs, (g_ref, dh, dl) = refs[12:-3], refs[-3:]
    chans = prev_ref.shape[0] // 2
    cols = prev_ref.shape[1]
    last = rows - 1
    mm, nt = ((1,), (0,)), ((1,), (1,))
    tall = [slice(k * chans, (k + 1) * chans) for k in range(3)]
    x_rim = {0: (0, halves(prev_ref[:chans, :])), 2: (last, halves(next_ref[:chans, :]))}
    c_rim = {2: (0, halves(prev_ref[chans:, :])), 0: (last, halves(next_ref[chans:, :]))}
    pre_rim = {
        row: dot3(fh[:, tall[a]], fl[:, tall[a]], *rim, mm) for a, (row, rim) in x_rim.items()
    }
    back_rim = {
        row: dot3(gh[:, tall[a]], gl[:, tall[a]], *rim, mm) for a, (row, rim) in c_rim.items()
    }
    dpres = []
    for row in range(rows):
        wide = slice(row * cols, (row + 1) * cols)

        def summed(ref, rim, k):
            value = ref[tall[k], wide]
            return value + rim[row][tall[k], :] if row in rim else value

        pre = scale * (
            summed(pre_ref, pre_rim, 1)
            + moved(summed(pre_ref, pre_rim, 0), -1)
            + moved(summed(pre_ref, pre_rim, 2), 1)
        )
        dhidden = scale * (
            summed(back_ref, back_rim, 1)
            + moved(summed(back_ref, back_rim, 0), 1)
            + moved(summed(back_ref, back_rim, 2), -1)
        )
        sig = jax.nn.sigmoid(pre)
        hidden = pre * sig
        dpres.append(dhidden * sig * (1.0 + pre * (1.0 - sig)))
        for b, value in enumerate((moved(hidden, -1), hidden, moved(hidden, 1))):
            put(dh, dl, b, row, value)
    grad2 = dot3(dh[...], dl[...], ch[...], cl[...], nt)
    for a in range(3):
        part = grad2[:, tall[a]]
        if a in c_rim:
            row, rim = c_rim[a]
            wide = slice(row * cols, (row + 1) * cols)
            part = part + dot3(dh[:, wide], dl[:, wide], *rim, nt)
        for b in range(3):
            t = 3 * a + b
            g_ref[1, t * chans : (t + 1) * chans, :] = scale * part[tall[b], :]
    for row, dpre in enumerate(dpres):
        for b, value in enumerate((moved(dpre, 1), dpre, moved(dpre, -1))):
            put(dh, dl, b, row, value)
    grad1 = dot3(xh[...], xl[...], dh[...], dl[...], nt)
    for a in range(3):
        part = grad1[tall[a], :]
        if a in x_rim:
            row, rim = x_rim[a]
            wide = slice(row * cols, (row + 1) * cols)
            part = part + dot3(*rim, dh[:, wide], dl[:, wide], nt)
        for b in range(3):
            t = 3 * a + b
            g_ref[0, t * chans : (t + 1) * chans, :] = scale * part[:, tall[b]]
    band = lax.axis_index("band")
    size = g_ref.shape[1] // n_band
    for k in range(n_band):
        start = lax.bitwise_xor(band, k) * size
        for c, (off, height) in enumerate(cuts):
            at = pl.ds(pl.multiple_of(start + off, 8), height)
            for layer in range(2):
                outs[c * n_band + k][layer] = g_ref[layer, at, :]


def sum_kernel(n_band, *refs):
    parts, (keep_ref, give_ref) = refs[:n_band], refs[n_band:]
    mine = lax.axis_index("image") % 2
    for out, layer in ((keep_ref, mine), (give_ref, 1 - mine)):
        total = parts[0][layer]
        for part in parts[1:]:
            total = total + part[layer]
        out[...] = total


def pack_kernel(n_pair, keep_ref, other_ref, *outs):
    image = lax.axis_index("image")
    mine = image % 2
    pair = image // 2
    size = keep_ref.shape[0] // n_pair
    for k, out in enumerate(outs):
        start = pl.multiple_of(lax.bitwise_xor(pair, k) * size, 8)
        out[mine] = keep_ref[pl.ds(start, size), :]
        out[1 - mine] = other_ref[pl.ds(start, size), :]


def gram_kernel(n_pair, cuts, *refs):
    parts, (out, held) = refs[:-2], refs[-2:]
    pair = lax.axis_index("image") // 2
    for c, (off, height) in enumerate(cuts):
        for k in range(n_pair):
            at = lax.bitwise_xor(pair, k) * 2
            for j in range(2):
                held[at + j, off : off + height, :] = parts[c * n_pair + k][j]
    count = 2 * n_pair
    col = lax.broadcasted_iota(jnp.int32, out.shape, 1)
    total = jnp.zeros(out.shape, F32)
    for i in range(count):
        for j in range(i, count):
            value = jnp.sum(held[i] * held[j], keepdims=True)
            total = jnp.where((col == i * count + j) | (col == j * count + i), value, total)
    out[...] = total


def merge_kernel(n_pair, n_band, cuts, sums_ref, *refs):
    parts, out = refs[:-1], refs[-1]
    image = lax.axis_index("image")
    mine = image % 2
    pair = image // 2
    count = 2 * n_pair
    sums = sums_ref[...]
    lanes = sums.shape[1]
    device = lax.broadcasted_iota(jnp.int32, sums.shape, 0)
    same = ((device // n_band) % 2) == mine
    flat = jnp.sum(jnp.where(same, sums, 0.0), 0, keepdims=True)
    row = lax.broadcasted_iota(jnp.int32, (count, lanes), 0)
    col = lax.broadcasted_iota(jnp.int32, (count, lanes), 1)
    gram = jnp.broadcast_to(flat, (count, lanes))
    wide = gram
    for i in range(1, count):
        gram = jnp.where(row == i, pltpu.roll(wide, lanes - i * count, 1), gram)
    gram = jnp.where(col < count, gram, 0.0)

    def swap(value, axis, step):
        size = value.shape[axis]
        index = row if axis == 0 else col
        return jnp.where(
            (index & step) != 0,
            pltpu.roll(value, step, axis),
            pltpu.roll(value, size - step, axis),
        )

    weight = jnp.ones((count, 1), F32)
    step = 1
    while step < count:
        own = jnp.where(row == col, gram, 0.0)
        cross = jnp.where((row ^ step) == col, gram, 0.0)
        down = 1.0 - jnp.sum(cross, 1, keepdims=True) / (
            2.0 * (jnp.sum(own, 1, keepdims=True) + 1e-06)
        )
        along = 1.0 - jnp.sum(cross, 0, keepdims=True) / (
            2.0 * (jnp.sum(own, 0, keepdims=True) + 1e-06)
        )
        weight = weight * down
        gram = gram * down * along
        gram = gram + swap(gram, 0, step)
        gram = gram + swap(gram, 1, step)
        step *= 2
    place = lax.broadcasted_iota(jnp.int32, weight.shape, 0)
    factors = {}
    for k in range(n_pair):
        at = lax.bitwise_xor(pair, k) * 2
        for j in range(2):
            factors[k, j] = jnp.sum(jnp.where(place == at + j, weight, 0.0), keepdims=True)
    for c, (off, height) in enumerate(cuts):
        total = jnp.zeros((height, out.shape[1]), F32)
        for k in range(n_pair):
            for j in range(2):
                total = total + factors[k, j] * parts[c * n_pair + k][j]
        out[off : off + height, :] = total


def gather_kernel(n_pair, cuts, *refs):
    parts, out = refs[:n_pair], refs[n_pair]
    pair = lax.axis_index("image") // 2
    for off, height in cuts:
        for k, part in enumerate(parts):
            start = off * n_pair + lax.bitwise_xor(pair, k) * height
            out[pl.ds(pl.multiple_of(start, 8), height), :] = part[off : off + height, :]


def final_kernel(n_band, chans, rates_ref, f_ref, *refs):
    own, others = refs[:n_band], refs[n_band : 2 * n_band]
    out = refs[2 * n_band]
    held = refs[2 * n_band + 1]
    mine = lax.axis_index("image") % 2
    band = lax.axis_index("band")
    size = own[0].shape[0]
    for k in range(n_band):
        start = pl.multiple_of(lax.bitwise_xor(band, k) * size, 8)
        held[mine, pl.ds(start, size), :] = own[k][...]
        held[1 - mine, pl.ds(start, size), :] = others[k][...]
    for layer in range(2):
        rate = rates_ref[layer]
        for t in range(9):
            at = pl.ds(t, chans, stride=9)
            out[0, layer, at, :] = (
                f_ref[layer, at, :] - rate * held[layer, t * chans : (t + 1) * chans, :]
            )


def xor_route(count, k):
    return [(i, i ^ k) for i in range(count)]


def swapped(value, axis, k):
    return lax.ppermute(value, axis, xor_route(lax.axis_size(axis), k))


def fast(images, cotangent, filters, rates):
    _, chans, rows, cols = images.shape
    n_band = lax.axis_size("band")
    n_image = lax.axis_size("image")
    n_pair = n_image // 2
    kdim = filters.shape[1]
    block = kdim // n_band
    slot = block // n_pair
    scale = kdim ** (-0.5)
    x = images.reshape(chans * rows, cols)
    cot = cotangent.reshape(chans * rows, cols)
    down, up = pl.pallas_call(
        edges_kernel,
        out_shape=[jax.ShapeDtypeStruct((2 * chans, cols), F32)] * 2,
        in_specs=[pl.BlockSpec(memory_space=pl.ANY)] * 2,
        scratch_shapes=[pltpu.VMEM(x.shape, F32)] * 2 + [pltpu.SemaphoreType.DMA((2,))],
        compiler_params=pltpu.CompilerParams(vmem_limit_bytes=60 * 2**20),
    )(x, cot)
    fwd = [(i, i + 1) for i in range(n_band - 1)]
    bwd = [(j, i) for i, j in fwd]
    before = lax.ppermute(down, "band", fwd)
    after = lax.ppermute(up, "band", bwd)
    tall, wide = 3 * chans, rows * cols
    inner = pl.pallas_call(
        functools.partial(inner_kernel, rows),
        out_shape=[jax.ShapeDtypeStruct((tall, wide), BF16)] * 4
        + [jax.ShapeDtypeStruct((tall, tall), BF16)] * 4
        + [jax.ShapeDtypeStruct((tall, wide), F32)] * 2,
        cost_estimate=pl.CostEstimate(
            flops=12 * tall * tall * wide, bytes_accessed=8 * kdim * chans, transcendentals=0
        ),
        compiler_params=pltpu.CompilerParams(vmem_limit_bytes=40 * 2**20),
    )(x, cot, filters)
    tiles = slot // 8
    first = 8 * ((tiles + 1) // 2)
    slots = [(0, first)] + ([(first, slot - first)] if first < slot else [])
    cuts = [(off * n_pair, height * n_pair) for off, height in slots]
    parts = call(
        functools.partial(grads_kernel, rows, scale, n_band, cuts),
        [(2, height, chans) for _, height in cuts for _ in range(n_band)],
        [
            pltpu.VMEM((2, kdim, chans), F32),
            pltpu.VMEM((tall, wide), BF16),
            pltpu.VMEM((tall, wide), BF16),
        ],
    )(before, after, *inner)
    sent = []
    for c in range(len(cuts)):
        mine = parts[c * n_band : (c + 1) * n_band]
        sent.append([mine[0]] + [swapped(mine[k], "band", k) for k in range(1, n_band)])
    slices = []
    for c, (_, height) in enumerate(cuts):
        keep, give = call(functools.partial(sum_kernel, n_band), [(height, chans)] * 2)(*sent[c])
        other = swapped(give, "image", 1)
        packed = call(
            functools.partial(pack_kernel, n_pair), [(2, height // n_pair, chans)] * n_pair
        )(keep, other)
        slices += [packed[0]] + [swapped(packed[k], "image", 2 * k) for k in range(1, n_pair)]
    (gram,) = call(
        functools.partial(gram_kernel, n_pair, slots),
        [(1, 128)],
        [pltpu.VMEM((n_image, slot, chans), F32)],
    )(*slices)
    sums = jnp.broadcast_to(gram, (n_image * n_band, gram.shape[1]))
    sums = lax.all_to_all(sums, ("image", "band"), 0, 0, tiled=True)
    (mine,) = call(
        functools.partial(merge_kernel, n_pair, n_band, slots), [(slot, chans)]
    )(sums, *slices)
    pieces = [mine] + [
        lax.ppermute(mine, "image", xor_route(n_image, 2 * k)) for k in range(1, n_pair)
    ]
    (mine,) = call(functools.partial(gather_kernel, n_pair, slots), [(block, chans)])(*pieces)
    own = [mine] + [
        lax.ppermute(mine, "band", xor_route(n_band, k)) for k in range(1, n_band)
    ]
    others = [lax.ppermute(piece, "image", xor_route(n_image, 1)) for piece in own]
    out = pl.pallas_call(
        functools.partial(final_kernel, n_band, chans),
        out_shape=jax.ShapeDtypeStruct((1,) + filters.shape, F32),
        in_specs=[pl.BlockSpec(memory_space=pltpu.SMEM)]
        + [pl.BlockSpec(memory_space=pltpu.VMEM)] * (1 + 2 * n_band),
        scratch_shapes=[pltpu.VMEM(filters.shape, F32)],
        compiler_params=pltpu.CompilerParams(vmem_limit_bytes=48 * 2**20),
    )(rates, filters, *own, *others)
    return out


def with_rims(field):
    count = lax.axis_size("band")
    forward = [(i, i + 1) for i in range(count - 1)]
    backward = [(target, source) for source, target in forward]
    low = lax.ppermute(field[:, -1:], "band", forward)
    high = lax.ppermute(field[:, :1], "band", backward)
    extended = jnp.concatenate([low, field, high], axis=1)
    return jnp.pad(extended, ((0, 0), (0, 0), (1, 1)))


def taps(padded, rows, cols, flip=False):
    chans = padded.shape[0]
    at = (2, 1, 0) if flip else (0, 1, 2)
    pieces = [padded[:, dr : dr + rows, dc : dc + cols] for dr in at for dc in at]
    return jnp.stack(pieces, axis=1).reshape(chans, 9, rows * cols)


def plain(images, cotangent, filters, rates):
    feats, cot = images[0], cotangent[0]
    chans, rows, cols = feats.shape
    scale = (9 * chans) ** (-0.5)
    patch_one = taps(with_rims(feats), rows, cols).reshape(9 * chans, rows * cols)
    pre = scale * jnp.einsum("kc,kp->cp", filters[0], patch_one, precision=HIGH)
    hidden = jax.nn.silu(pre).reshape(chans, rows, cols)
    patch_two = taps(with_rims(hidden), rows, cols).reshape(9 * chans, rows * cols)
    back = taps(with_rims(cot), rows, cols, flip=True)
    flat_cot = cot.reshape(chans, rows * cols)
    grad_two = scale * jnp.einsum("kp,cp->kc", patch_two, flat_cot, precision=HIGH)
    weight_two = filters[1].reshape(chans, 9, chans)
    dhidden = scale * jnp.einsum("itc,ctp->ip", weight_two, back, precision=HIGH)
    sig = jax.nn.sigmoid(pre)
    dpre = dhidden * sig * (1.0 + pre * (1.0 - sig))
    grad_one = scale * jnp.einsum("kp,cp->kc", patch_one, dpre, precision=HIGH)
    block = lax.psum_scatter(
        jnp.stack([grad_one, grad_two]), "band", scatter_dimension=1, tiled=True
    )
    count = lax.axis_size("image")
    for level in range(count.bit_length() - 1):
        other = lax.ppermute(block, "image", xor_route(count, 1 << level))
        inner, own_sq, other_sq = lax.psum(
            tuple(jnp.sum(v, axis=(1, 2)) for v in (block * other, block * block, other * other)),
            "band",
        )
        low = (1.0 - inner / (2.0 * (own_sq + 1e-06)))[:, None, None]
        high = (1.0 - inner / (2.0 * (other_sq + 1e-06)))[:, None, None]
        block = low * block + high * other
    height = block.shape[1]
    mine = lax.dynamic_slice_in_dim(filters, lax.axis_index("band") * height, height, 1)
    fresh = (mine - rates[:, None, None] * block)[None]
    return lax.all_gather(fresh, "band", axis=2, tiled=True)


def local(images, cotangent, filters, rates):
    n_band = lax.axis_size("band")
    n_image = lax.axis_size("image")
    kdim = filters.shape[1]
    fits = (
        4 <= n_image and n_image**2 <= 128
        and n_image & (n_image - 1) == 0
        and n_band & (n_band - 1) == 0
        and kdim % (n_band * (n_image // 2) * 8) == 0
    )
    return (fast if fits else plain)(images, cotangent, filters, rates)


def solution(mesh):
    in_specs = (P("image", None, "band", None), P("image", None, "band", None), P(), P())
    out_specs = P("image", None, None, None)
    return jax.shard_map(local, mesh=mesh, in_specs=in_specs, out_specs=out_specs, check_vma=False)
```

```python
import functools

import jax
import jax.numpy as jnp
from jax import lax
from jax.experimental import pallas as pl
from jax.experimental.pallas import tpu as pltpu
from jax.sharding import PartitionSpec as P


HIGH = lax.Precision.HIGHEST
F32 = jnp.float32
BF16 = jnp.bfloat16


AXES = ("pair", "core", "half", "lo")


def call(body, outs, scratch=(), flops=0):
    outs = [o if isinstance(o, jax.ShapeDtypeStruct) else jax.ShapeDtypeStruct(o, F32) for o in outs]
    return pl.pallas_call(
        body,
        out_shape=outs,
        scratch_shapes=list(scratch),
        cost_estimate=pl.CostEstimate(flops=flops, bytes_accessed=flops // 500, transcendentals=0),
        compiler_params=pltpu.CompilerParams(vmem_limit_bytes=40 * 2**20),
    )


def halves(value):
    high = value.astype(BF16)
    return high, (value - high.astype(F32)).astype(BF16)


def dot3(ah, al, bh, bl, dims):
    def one(a, b):
        return lax.dot_general(a, b, (dims, ((), ())), preferred_element_type=F32)

    return one(ah, bh) + (one(ah, bl) + one(al, bh))


def moved(value, step):
    cols = value.shape[-1]
    col = lax.broadcasted_iota(jnp.int32, value.shape, value.ndim - 1)
    if step > 0:
        return jnp.where(col == cols - 1, 0.0, pltpu.roll(value, cols - 1, 1))
    return jnp.where(col == 0, 0.0, pltpu.roll(value, 1, 1))


def put(high_ref, low_ref, at, row, value):
    high, low = halves(value)
    rows, cols = value.shape
    part = (slice(at * rows, (at + 1) * rows), slice(row * cols, (row + 1) * cols))
    high_ref[part] = high
    low_ref[part] = low


def filter_kernel(f_ref, fh, fl, gh, gl, taps_ref):
    lo = lax.axis_index("lo")
    chans = f_ref.shape[2]
    mine = fh.shape[0] // 3
    rows = pl.ds(pl.multiple_of(lo * mine, 8), mine)
    for a in range(3):
        for b in range(3):
            t = 3 * a + b
            at = pl.ds(t, chans, stride=9)
            taps_ref[0, t] = f_ref[0, at, :].T
            taps_ref[1, t] = f_ref[1, at, :]
            put(fh, fl, b, a, taps_ref[0, t, rows, :])
            put(gh, gl, b, a, taps_ref[1, t, rows, :])


def edge_kernel(own_ref, *refs):
    parts, out = refs[:-1], refs[-1]
    core, lo = lax.axis_index("core"), lax.axis_index("lo")
    kept = core == lax.axis_index("half")
    count = len(parts)
    chans = out.shape[0]
    rows = own_ref.shape[0] // chans
    place = jnp.where(core == 0, count - 1, 0)
    for k, part in enumerate(parts):
        for c, row in ((0, rows - 1), (1, 0)):
            here = (lax.bitwise_xor(lo, k) == place) & (core == c)
            at = pl.ds(row, chans, stride=rows)
            if k == 0:

                @pl.when(here & kept)
                def _():
                    out[...] = own_ref[at, :]

                here = here & jnp.logical_not(kept)

            @pl.when(here)
            def _():
                out[...] = part[at, :]


def rows_kernel(flip, own_ref, *refs):
    parts, (fh, fl, vh, vl, out, raw) = refs[:-6], refs[-6:]
    lo = lax.axis_index("lo")
    kept = lax.axis_index("core") == lax.axis_index("half")
    chans = raw.shape[1]
    cols = raw.shape[2]
    rows = own_ref.shape[0] // chans
    total = raw.shape[0]

    def take(ref, at):
        for row in range(rows):
            raw[at + row] = ref[pl.ds(row, chans, stride=rows), :]

    for k, part in enumerate(parts):
        at = lax.bitwise_xor(lo, k) * rows
        if k:
            take(part, at)
            continue

        @pl.when(kept)
        def _():
            take(own_ref, at)

        @pl.when(jnp.logical_not(kept))
        def _():
            take(part, at)

    for a in range(3):
        step = 1 - a if flip else a - 1
        for row in range(total):
            value = raw[row + step] if 0 <= row + step < total else jnp.zeros((chans, cols), F32)
            put(vh, vl, a, row, value)
    out[...] = dot3(fh[...], fl[...], vh[...], vl[...], ((1,), (0,)))


def grads_kernel(total, scale, *refs):
    x_edge, c_edge, xh, xl, ch, cl, fh, fl, gh, gl, pre_ref, back_ref = refs[:12]
    (keep_ref, give_ref), (g_ref, dh, dl) = refs[12:14], refs[14:]
    chans, cols = x_edge.shape
    mine = fh.shape[0] // 3
    core = lax.axis_index("core")
    last = total - 1
    mm, nt = ((1,), (0,)), ((1,), (1,))
    tall = [slice(k * chans, (k + 1) * chans) for k in range(3)]
    part_of = [slice(k * mine, (k + 1) * mine) for k in range(3)]

    def rims(edge, first, final):
        before = halves(jnp.where(core == 1, edge[...], 0.0))
        after = halves(jnp.where(core == 0, edge[...], 0.0))
        return {first: (0, before), final: (last, after)}

    x_rim = rims(x_edge, 0, 2)
    c_rim = rims(c_edge, 2, 0)
    pre_rim = {
        row: dot3(fh[:, tall[a]], fl[:, tall[a]], *rim, mm) for a, (row, rim) in x_rim.items()
    }
    back_rim = {
        row: dot3(gh[:, tall[a]], gl[:, tall[a]], *rim, mm) for a, (row, rim) in c_rim.items()
    }
    for row in range(total):
        wide = slice(row * cols, (row + 1) * cols)

        def summed(ref, rim, k):
            value = ref[part_of[k], wide]
            return value + rim[row][part_of[k], :] if row in rim else value

        pre = scale * (
            summed(pre_ref, pre_rim, 1)
            + moved(summed(pre_ref, pre_rim, 0), -1)
            + moved(summed(pre_ref, pre_rim, 2), 1)
        )
        dhidden = scale * (
            summed(back_ref, back_rim, 1)
            + moved(summed(back_ref, back_rim, 0), 1)
            + moved(summed(back_ref, back_rim, 2), -1)
        )
        sig = jax.nn.sigmoid(pre)
        hidden = pre * sig
        dpre = dhidden * sig * (1.0 + pre * (1.0 - sig))
        for b, value in enumerate((moved(dpre, 1), dpre, moved(dpre, -1))):
            put(dh.at[0], dl.at[0], b, row, value)
        for b, value in enumerate((moved(hidden, -1), hidden, moved(hidden, 1))):
            put(dh.at[1], dl.at[1], b, row, value)
    for layer, (vh, vl, rim_of) in enumerate(((xh, xl, x_rim), (ch, cl, c_rim))):
        grad = dot3(dh[layer], dl[layer], vh[...], vl[...], nt)
        for a in range(3):
            part = grad[:, tall[a]]
            if a in rim_of:
                row, rim = rim_of[a]
                wide = slice(row * cols, (row + 1) * cols)
                part = part + dot3(dh[layer, :, wide], dl[layer, :, wide], *rim, nt)
            for b in range(3):
                t = 3 * a + b
                g_ref[layer, t * mine : (t + 1) * mine, :] = scale * part[part_of[b], :]
    keep_ref[...] = g_ref[core]
    give_ref[...] = g_ref[1 - core]


def gram_kernel(v_ref, out):
    count = v_ref.shape[0]
    col = lax.broadcasted_iota(jnp.int32, out.shape, 1)
    total = jnp.zeros(out.shape, F32)
    for i in range(count):
        for j in range(i, count):
            value = jnp.sum(v_ref[i] * v_ref[j], keepdims=True)
            total = jnp.where((col == i * count + j) | (col == j * count + i), value, total)
    out[...] = total


def merge_kernel(n_band, sums_ref, v_ref, out):
    core = lax.axis_index("core")
    count = v_ref.shape[0]
    sums = sums_ref[...]
    lanes = sums.shape[1]
    device = lax.broadcasted_iota(jnp.int32, sums.shape, 0)
    same = ((device // n_band) % 2) == core
    flat = jnp.sum(jnp.where(same, sums, 0.0), 0, keepdims=True)
    row = lax.broadcasted_iota(jnp.int32, (count, lanes), 0)
    col = lax.broadcasted_iota(jnp.int32, (count, lanes), 1)
    gram = jnp.broadcast_to(flat, (count, lanes))
    wide = gram
    for i in range(1, count):
        gram = jnp.where(row == i, pltpu.roll(wide, lanes - i * count, 1), gram)
    gram = jnp.where(col < count, gram, 0.0)

    def swap(value, axis, step):
        size = value.shape[axis]
        index = row if axis == 0 else col
        return jnp.where(
            (index & step) != 0,
            pltpu.roll(value, step, axis),
            pltpu.roll(value, size - step, axis),
        )

    weight = jnp.ones((count, 1), F32)
    step = 1
    while step < count:
        own = jnp.where(row == col, gram, 0.0)
        cross = jnp.where((row ^ step) == col, gram, 0.0)
        down = 1.0 - jnp.sum(cross, 1, keepdims=True) / (
            2.0 * (jnp.sum(own, 1, keepdims=True) + 1e-06)
        )
        along = 1.0 - jnp.sum(cross, 0, keepdims=True) / (
            2.0 * (jnp.sum(own, 0, keepdims=True) + 1e-06)
        )
        weight = weight * down
        gram = gram * down * along
        gram = gram + swap(gram, 0, step)
        gram = gram + swap(gram, 1, step)
        step *= 2
    total = jnp.zeros(out.shape, F32)
    for i in range(count):
        total = total + weight[i : i + 1, :] * v_ref[i]
    out[...] = total


def gather_kernel(*refs):
    parts, out = refs[:-1], refs[-1]
    pair = lax.axis_index("pair")
    size = parts[0].shape[0]
    for k, part in enumerate(parts):
        start = pl.multiple_of(lax.bitwise_xor(pair, k) * size, 8)
        out[pl.ds(start, size), :] = part[...]


def final_kernel(n_pair, n_lo, rates_ref, f_ref, *refs):
    n_band = 2 * n_lo
    own, others = refs[:n_band], refs[n_band : 2 * n_band]
    out, held = refs[2 * n_band :]
    core = lax.axis_index("core")
    band = lax.axis_index("half") * n_lo + lax.axis_index("lo")
    size = own[0].shape[0] // n_pair
    chans = f_ref.shape[2]
    mine = chans // n_lo
    for k in range(n_band):
        place = lax.bitwise_xor(band, k)
        half, lo = place // n_lo, place % n_lo
        for p in range(n_pair):
            to = pl.ds(pl.multiple_of((2 * p + half) * size, 8), size)
            at = slice(p * size, (p + 1) * size)
            held[core, lo, to, :] = own[k][at, :]
            held[1 - core, lo, to, :] = others[k][at, :]
    for layer in range(2):
        rate = rates_ref[layer]
        for t in range(9):
            at = pl.ds(t, chans, stride=9)
            value = held[layer, :, t * mine : (t + 1) * mine, :].reshape(chans, chans)
            if layer == 0:
                value = value.T
            out[0, layer, at, :] = f_ref[layer, at, :] - rate * value


def xor_route(count, k):
    return [(i, i ^ k) for i in range(count)]


def swapped(value, axis, k):
    return lax.ppermute(value, axis, xor_route(lax.axis_size(axis), k))


def inputs_of(value, n_lo):
    def at(core, half, lo):
        return (core * 2 + half) * n_lo + lo

    found = []
    for k in range(n_lo - 1, -1, -1):
        route = [
            (at(core, half, lo), at(half, core, lo ^ k))
            for core in range(2)
            for half in range(2)
            for lo in range(n_lo)
            if k or core != half
        ]
        found.append(lax.ppermute(value, ("core", "half", "lo"), route))
    return found[::-1]


def fast(images, cotangent, filters, rates):
    _, chans, rows, cols = images.shape
    n_pair, n_lo = lax.axis_size("pair"), lax.axis_size("lo")
    n_image, n_band = 2 * n_pair, 2 * n_lo
    kdim = filters.shape[1]
    mine = chans // n_lo
    total = n_lo * rows
    slot = 9 * mine // n_image
    flat = (chans * rows, cols)
    bf = lambda *shape: jax.ShapeDtypeStruct(shape, BF16)
    tall, thin, wide = 3 * chans, 3 * mine, total * cols
    xs = inputs_of(images, n_lo)
    cs = inputs_of(cotangent, n_lo)
    xs = [v.reshape(flat) for v in [images] + xs]
    cs = [v.reshape(flat) for v in [cotangent] + cs]
    fh, fl, gh, gl = call(
        filter_kernel, [bf(thin, tall)] * 4, [pltpu.VMEM((2, 9, chans, chans), F32)]
    )(filters)
    (edge,) = call(edge_kernel, [(chans, cols)])(*xs)
    x_edge = swapped(edge, "core", 1)
    raw = [pltpu.VMEM((total, chans, cols), F32)]
    work = 6 * thin * tall * wide
    outs = [bf(tall, wide)] * 2 + [(thin, wide)]
    xh, xl, pre = call(
        functools.partial(rows_kernel, False), outs, raw, flops=work
    )(*xs, fh, fl)
    (edge,) = call(edge_kernel, [(chans, cols)])(*cs)
    c_edge = swapped(edge, "core", 1)
    ch, cl, back = call(
        functools.partial(rows_kernel, True), outs, raw, flops=work
    )(*cs, gh, gl)
    keep, give = call(
        functools.partial(grads_kernel, total, kdim ** (-0.5)),
        [(9 * mine, chans)] * 2,
        [
            pltpu.VMEM((2, 9 * mine, chans), F32),
            pltpu.VMEM((2, thin, wide), BF16),
            pltpu.VMEM((2, thin, wide), BF16),
        ],
        flops=2 * work,
    )(x_edge, c_edge, xh, xl, ch, cl, fh, fl, gh, gl, pre, back)
    whole = keep + swapped(give, "core", 1)
    slices = lax.all_to_all(
        whole.reshape(n_image, slot, chans), ("pair", "half"), 0, 0, tiled=True
    )
    (gram,) = call(gram_kernel, [(1, 128)])(slices)
    sums = jnp.broadcast_to(gram, (n_image * n_band, gram.shape[1]))
    sums = lax.all_to_all(sums, AXES, 0, 0, tiled=True)
    (merged,) = call(functools.partial(merge_kernel, n_band), [(slot, chans)])(
        sums, slices
    )
    pieces = [merged] + [swapped(merged, "pair", k) for k in range(1, n_pair)]
    (part,) = call(gather_kernel, [(n_pair * slot, chans)])(*pieces)
    own = [part] + [swapped(part, ("half", "lo"), k) for k in range(1, n_band)]
    others = [swapped(piece, "core", 1) for piece in own]
    return pl.pallas_call(
        functools.partial(final_kernel, n_pair, n_lo),
        out_shape=jax.ShapeDtypeStruct((1,) + filters.shape, F32),
        in_specs=[pl.BlockSpec(memory_space=pltpu.SMEM)]
        + [pl.BlockSpec(memory_space=pltpu.VMEM)] * (1 + 2 * n_band),
        scratch_shapes=[pltpu.VMEM((2, n_lo, 9 * mine, chans), F32)],
        compiler_params=pltpu.CompilerParams(vmem_limit_bytes=40 * 2**20),
    )(rates, filters, *own, *others)


def with_rims(field):
    count = lax.axis_size("band")
    forward = [(i, i + 1) for i in range(count - 1)]
    backward = [(target, source) for source, target in forward]
    low = lax.ppermute(field[:, -1:], "band", forward)
    high = lax.ppermute(field[:, :1], "band", backward)
    extended = jnp.concatenate([low, field, high], axis=1)
    return jnp.pad(extended, ((0, 0), (0, 0), (1, 1)))


def taps(padded, rows, cols, flip=False):
    chans = padded.shape[0]
    at = (2, 1, 0) if flip else (0, 1, 2)
    pieces = [padded[:, dr : dr + rows, dc : dc + cols] for dr in at for dc in at]
    return jnp.stack(pieces, axis=1).reshape(chans, 9, rows * cols)


def plain(images, cotangent, filters, rates):
    feats, cot = images[0], cotangent[0]
    chans, rows, cols = feats.shape
    scale = (9 * chans) ** (-0.5)
    patch_one = taps(with_rims(feats), rows, cols).reshape(9 * chans, rows * cols)
    pre = scale * jnp.einsum("kc,kp->cp", filters[0], patch_one, precision=HIGH)
    hidden = jax.nn.silu(pre).reshape(chans, rows, cols)
    patch_two = taps(with_rims(hidden), rows, cols).reshape(9 * chans, rows * cols)
    back = taps(with_rims(cot), rows, cols, flip=True)
    flat_cot = cot.reshape(chans, rows * cols)
    grad_two = scale * jnp.einsum("kp,cp->kc", patch_two, flat_cot, precision=HIGH)
    weight_two = filters[1].reshape(chans, 9, chans)
    dhidden = scale * jnp.einsum("itc,ctp->ip", weight_two, back, precision=HIGH)
    sig = jax.nn.sigmoid(pre)
    dpre = dhidden * sig * (1.0 + pre * (1.0 - sig))
    grad_one = scale * jnp.einsum("kp,cp->kc", patch_one, dpre, precision=HIGH)
    block = lax.psum_scatter(
        jnp.stack([grad_one, grad_two]), "band", scatter_dimension=1, tiled=True
    )
    count = lax.axis_size("image")
    for level in range(count.bit_length() - 1):
        other = lax.ppermute(block, "image", xor_route(count, 1 << level))
        inner, own_sq, other_sq = lax.psum(
            tuple(jnp.sum(v, axis=(1, 2)) for v in (block * other, block * block, other * other)),
            "band",
        )
        low = (1.0 - inner / (2.0 * (own_sq + 1e-06)))[:, None, None]
        high = (1.0 - inner / (2.0 * (other_sq + 1e-06)))[:, None, None]
        block = low * block + high * other
    height = block.shape[1]
    mine = lax.dynamic_slice_in_dim(filters, lax.axis_index("band") * height, height, 1)
    fresh = (mine - rates[:, None, None] * block)[None]
    return lax.all_gather(fresh, "band", axis=2, tiled=True)


def power_of_two(n):
    return n & (n - 1) == 0


def solution(mesh):
    n_image, n_band = mesh.shape["image"], mesh.shape["band"]

    def step(images, cotangent, filters, rates):
        chans = images.shape[1]
        if (
            4 <= n_image
            and n_image**2 <= 128
            and 4 <= n_band
            and power_of_two(n_image)
            and power_of_two(n_band)
            and (9 * chans) % (n_band // 2 * n_image * 8) == 0
        ):
            shape = (n_image // 2, 2, 2, n_band // 2)
            split = jax.sharding.Mesh(mesh.devices.reshape(shape), AXES)
            image, band = ("pair", "core"), ("half", "lo")

            def body(*args):
                return fast(*args)

        else:
            split, image, band, body = mesh, "image", "band", plain
        whole = jax.shard_map(
            body,
            mesh=split,
            in_specs=(P(image, None, band, None), P(image, None, band, None), P(), P()),
            out_specs=P(image, None, None, None),
            check_vma=False,
        )
        return whole(images, cotangent, filters, rates)

    return step
```

```python
import functools

import jax
import jax.numpy as jnp
from jax import lax
from jax.experimental import pallas as pl
from jax.experimental.pallas import tpu as pltpu
from jax.sharding import PartitionSpec as P


HIGH = lax.Precision.HIGHEST
F32 = jnp.float32
BF16 = jnp.bfloat16


AXES = ("pair", "core", "half", "lo")


def call(body, outs, scratch=(), flops=0):
    outs = [o if isinstance(o, jax.ShapeDtypeStruct) else jax.ShapeDtypeStruct(o, F32) for o in outs]
    return pl.pallas_call(
        body,
        out_shape=outs,
        scratch_shapes=list(scratch),
        cost_estimate=pl.CostEstimate(flops=flops, bytes_accessed=flops // 500, transcendentals=0),
        compiler_params=pltpu.CompilerParams(vmem_limit_bytes=40 * 2**20),
    )


def halves(value):
    high = value.astype(BF16)
    return high, (value - high.astype(F32)).astype(BF16)


def dot3(ah, al, bh, bl, dims):
    def one(a, b):
        return lax.dot_general(a, b, (dims, ((), ())), preferred_element_type=F32)

    return one(ah, bh) + (one(ah, bl) + one(al, bh))


def moved(value, step):
    cols = value.shape[-1]
    col = lax.broadcasted_iota(jnp.int32, value.shape, value.ndim - 1)
    if step > 0:
        return jnp.where(col == cols - 1, 0.0, pltpu.roll(value, cols - 1, 1))
    return jnp.where(col == 0, 0.0, pltpu.roll(value, 1, 1))


def put(high_ref, low_ref, at, row, value):
    high, low = halves(value)
    rows, cols = value.shape
    part = (slice(at * rows, (at + 1) * rows), slice(row * cols, (row + 1) * cols))
    high_ref[part] = high
    low_ref[part] = low


def filter_kernel(f_ref, fh, fl, gh, gl, taps_ref):
    lo = lax.axis_index("lo")
    chans = f_ref.shape[2]
    mine = fh.shape[0] // 3
    rows = pl.ds(pl.multiple_of(lo * mine, 8), mine)
    for a in range(3):
        for b in range(3):
            t = 3 * a + b
            at = pl.ds(t, chans, stride=9)
            taps_ref[0, t] = f_ref[0, at, :].T
            taps_ref[1, t] = f_ref[1, at, :]
            put(fh, fl, b, a, taps_ref[0, t, rows, :])
            put(gh, gl, b, a, taps_ref[1, t, rows, :])


def edge_kernel(own_ref, *refs):
    parts, out = refs[:-1], refs[-1]
    core, lo = lax.axis_index("core"), lax.axis_index("lo")
    kept = core == lax.axis_index("half")
    count = len(parts)
    chans = out.shape[0]
    rows = own_ref.shape[0] // chans
    place = jnp.where(core == 0, count - 1, 0)
    for k, part in enumerate(parts):
        for c, row in ((0, rows - 1), (1, 0)):
            here = (lax.bitwise_xor(lo, k) == place) & (core == c)
            at = pl.ds(row, chans, stride=rows)
            if k == 0:

                @pl.when(here & kept)
                def _():
                    out[...] = own_ref[at, :]

                here = here & jnp.logical_not(kept)

            @pl.when(here)
            def _():
                out[...] = part[at, :]


def rows_kernel(flip, own_ref, *refs):
    parts, (fh, fl, vh, vl, out, raw) = refs[:-6], refs[-6:]
    lo = lax.axis_index("lo")
    kept = lax.axis_index("core") == lax.axis_index("half")
    chans = raw.shape[1]
    cols = raw.shape[2]
    rows = own_ref.shape[0] // chans
    total = raw.shape[0]

    def take(ref, at):
        for row in range(rows):
            raw[at + row] = ref[pl.ds(row, chans, stride=rows), :]

    for k, part in enumerate(parts):
        at = lax.bitwise_xor(lo, k) * rows
        if k:
            take(part, at)
            continue

        @pl.when(kept)
        def _():
            take(own_ref, at)

        @pl.when(jnp.logical_not(kept))
        def _():
            take(part, at)

    for a in range(3):
        step = 1 - a if flip else a - 1
        for row in range(total):
            value = raw[row + step] if 0 <= row + step < total else jnp.zeros((chans, cols), F32)
            put(vh, vl, a, row, value)
    out[...] = dot3(fh[...], fl[...], vh[...], vl[...], ((1,), (0,)))


def rims(edge, first, final, last):
    core = lax.axis_index("core")
    before = halves(jnp.where(core == 1, edge[...], 0.0))
    after = halves(jnp.where(core == 0, edge[...], 0.0))
    return {first: (0, before), final: (last, after)}


def layer_grad(out, scale, dh, dl, vh, vl, rim_of):
    mine = dh.shape[0] // 3
    chans, cols = rim_of[0][1][0].shape
    grad = dot3(dh[...], dl[...], vh[...], vl[...], ((1,), (1,)))
    for a in range(3):
        part = grad[:, a * chans : (a + 1) * chans]
        if a in rim_of:
            row, rim = rim_of[a]
            wide = slice(row * cols, (row + 1) * cols)
            part = part + dot3(dh[:, wide], dl[:, wide], *rim, ((1,), (1,)))
        for b in range(3):
            t = 3 * a + b
            out[t * mine : (t + 1) * mine, :] = scale * part[b * mine : (b + 1) * mine, :]


def either(wanted, scale, out, x_edge, c_edge, xh, xl, ch, cl, dh, dl, last):

    @pl.when(wanted == 0)
    def _():
        layer_grad(out, scale, dh.at[0], dl.at[0], xh, xl, rims(x_edge, 0, 2, last))

    @pl.when(wanted == 1)
    def _():
        layer_grad(out, scale, dh.at[1], dl.at[1], ch, cl, rims(c_edge, 2, 0, last))


def give_kernel(total, scale, *refs):
    x_edge, c_edge, xh, xl, ch, cl, fh, fl, gh, gl, pre_ref, back_ref = refs[:12]
    give_ref, dh, dl = refs[12:]
    chans, cols = x_edge.shape
    mine = fh.shape[0] // 3
    mm = ((1,), (0,))
    part_of = [slice(k * mine, (k + 1) * mine) for k in range(3)]

    def rim_rows(wh, wl, rim_of):
        return {
            row: dot3(
                wh[:, a * chans : (a + 1) * chans], wl[:, a * chans : (a + 1) * chans], *rim, mm
            )
            for a, (row, rim) in rim_of.items()
        }

    pre_rim = rim_rows(fh, fl, rims(x_edge, 0, 2, total - 1))
    back_rim = rim_rows(gh, gl, rims(c_edge, 2, 0, total - 1))
    for row in range(total):
        wide = slice(row * cols, (row + 1) * cols)

        def summed(ref, rim, k):
            value = ref[part_of[k], wide]
            return value + rim[row][part_of[k], :] if row in rim else value

        pre = scale * (
            summed(pre_ref, pre_rim, 1)
            + moved(summed(pre_ref, pre_rim, 0), -1)
            + moved(summed(pre_ref, pre_rim, 2), 1)
        )
        dhidden = scale * (
            summed(back_ref, back_rim, 1)
            + moved(summed(back_ref, back_rim, 0), 1)
            + moved(summed(back_ref, back_rim, 2), -1)
        )
        sig = jax.nn.sigmoid(pre)
        hidden = pre * sig
        dpre = dhidden * sig * (1.0 + pre * (1.0 - sig))
        for b, value in enumerate((moved(dpre, 1), dpre, moved(dpre, -1))):
            put(dh.at[0], dl.at[0], b, row, value)
        for b, value in enumerate((moved(hidden, -1), hidden, moved(hidden, 1))):
            put(dh.at[1], dl.at[1], b, row, value)
    wanted = 1 - lax.axis_index("core")
    either(wanted, scale, give_ref, x_edge, c_edge, xh, xl, ch, cl, dh, dl, total - 1)


def keep_kernel(total, scale, x_edge, c_edge, xh, xl, ch, cl, dh, dl, keep_ref):
    wanted = lax.axis_index("core")
    either(wanted, scale, keep_ref, x_edge, c_edge, xh, xl, ch, cl, dh, dl, total - 1)


def gram_kernel(v_ref, out):
    count = v_ref.shape[0]
    col = lax.broadcasted_iota(jnp.int32, out.shape, 1)
    total = jnp.zeros(out.shape, F32)
    for i in range(count):
        for j in range(i, count):
            value = jnp.sum(v_ref[i] * v_ref[j], keepdims=True)
            total = jnp.where((col == i * count + j) | (col == j * count + i), value, total)
    out[...] = total


def merge_kernel(n_band, sums_ref, v_ref, out):
    core = lax.axis_index("core")
    count = v_ref.shape[0]
    sums = sums_ref[...]
    lanes = sums.shape[1]
    device = lax.broadcasted_iota(jnp.int32, sums.shape, 0)
    same = ((device // n_band) % 2) == core
    flat = jnp.sum(jnp.where(same, sums, 0.0), 0, keepdims=True)
    row = lax.broadcasted_iota(jnp.int32, (count, lanes), 0)
    col = lax.broadcasted_iota(jnp.int32, (count, lanes), 1)
    gram = jnp.broadcast_to(flat, (count, lanes))
    wide = gram
    for i in range(1, count):
        gram = jnp.where(row == i, pltpu.roll(wide, lanes - i * count, 1), gram)
    gram = jnp.where(col < count, gram, 0.0)

    def swap(value, axis, step):
        size = value.shape[axis]
        index = row if axis == 0 else col
        return jnp.where(
            (index & step) != 0,
            pltpu.roll(value, step, axis),
            pltpu.roll(value, size - step, axis),
        )

    weight = jnp.ones((count, 1), F32)
    step = 1
    while step < count:
        own = jnp.where(row == col, gram, 0.0)
        cross = jnp.where((row ^ step) == col, gram, 0.0)
        down = 1.0 - jnp.sum(cross, 1, keepdims=True) / (
            2.0 * (jnp.sum(own, 1, keepdims=True) + 1e-06)
        )
        along = 1.0 - jnp.sum(cross, 0, keepdims=True) / (
            2.0 * (jnp.sum(own, 0, keepdims=True) + 1e-06)
        )
        weight = weight * down
        gram = gram * down * along
        gram = gram + swap(gram, 0, step)
        gram = gram + swap(gram, 1, step)
        step *= 2
    total = jnp.zeros(out.shape, F32)
    for i in range(count):
        total = total + weight[i : i + 1, :] * v_ref[i]
    out[...] = total


def gather_kernel(*refs):
    parts, out = refs[:-1], refs[-1]
    pair = lax.axis_index("pair")
    size = parts[0].shape[0]
    for k, part in enumerate(parts):
        start = pl.multiple_of(lax.bitwise_xor(pair, k) * size, 8)
        out[pl.ds(start, size), :] = part[...]


def final_kernel(n_pair, n_lo, swap, rates_ref, f_ref, *refs):
    n_band = 2 * n_lo
    pieces = refs[:n_band]
    out, held, fresh, sem = refs[-4:]
    core = lax.axis_index("core")
    layer = 1 - core if swap else core
    band = lax.axis_index("half") * n_lo + lax.axis_index("lo")
    size = pieces[0].shape[0] // n_pair
    chans = f_ref.shape[2]
    mine = chans // n_lo
    for k, piece in enumerate(pieces):
        place = lax.bitwise_xor(band, k)
        half, lo = place // n_lo, place % n_lo
        for p in range(n_pair):
            to = pl.ds(pl.multiple_of((2 * p + half) * size, 8), size)
            held[lo, to, :] = piece[p * size : (p + 1) * size, :]
    for l in range(2):

        @pl.when(layer == l)
        def _():
            rate = rates_ref[l]
            for t in range(9):
                at = pl.ds(t, chans, stride=9)
                value = held[:, t * mine : (t + 1) * mine, :].reshape(chans, chans)
                if l == 0:
                    value = value.T
                fresh[at, :] = f_ref[l, at, :] - rate * value

    copy = pltpu.make_async_copy(fresh, out.at[0, layer], sem)
    copy.start()
    copy.wait()


def xor_route(count, k):
    return [(i, i ^ k) for i in range(count)]


def swapped(value, axis, k):
    return lax.ppermute(value, axis, xor_route(lax.axis_size(axis), k))


def inputs_of(value, n_lo):
    def at(core, half, lo):
        return (core * 2 + half) * n_lo + lo

    found = []
    for k in range(n_lo - 1, -1, -1):
        route = [
            (at(core, half, lo), at(half, core, lo ^ k))
            for core in range(2)
            for half in range(2)
            for lo in range(n_lo)
            if k or core != half
        ]
        found.append(lax.ppermute(value, ("core", "half", "lo"), route))
    return found[::-1]


def fast(images, cotangent, filters, rates):
    _, chans, rows, cols = images.shape
    n_pair, n_lo = lax.axis_size("pair"), lax.axis_size("lo")
    n_image, n_band = 2 * n_pair, 2 * n_lo
    kdim = filters.shape[1]
    mine = chans // n_lo
    total = n_lo * rows
    slot = 9 * mine // n_image
    flat = (chans * rows, cols)
    bf = lambda *shape: jax.ShapeDtypeStruct(shape, BF16)
    tall, thin, wide = 3 * chans, 3 * mine, total * cols
    xs = inputs_of(images, n_lo)
    cs = inputs_of(cotangent, n_lo)
    xs = [v.reshape(flat) for v in [images] + xs]
    cs = [v.reshape(flat) for v in [cotangent] + cs]
    fh, fl, gh, gl = call(
        filter_kernel, [bf(thin, tall)] * 4, [pltpu.VMEM((2, 9, chans, chans), F32)]
    )(filters)
    (edge,) = call(edge_kernel, [(chans, cols)])(*xs)
    x_edge = swapped(edge, "core", 1)
    raw = [pltpu.VMEM((total, chans, cols), F32)]
    work = 6 * thin * tall * wide
    outs = [bf(tall, wide)] * 2 + [(thin, wide)]
    xh, xl, pre = call(
        functools.partial(rows_kernel, False), outs, raw, flops=work
    )(*xs, fh, fl)
    (edge,) = call(edge_kernel, [(chans, cols)])(*cs)
    c_edge = swapped(edge, "core", 1)
    ch, cl, back = call(
        functools.partial(rows_kernel, True), outs, raw, flops=work
    )(*cs, gh, gl)
    scale = kdim ** (-0.5)
    rows_of = (x_edge, c_edge, xh, xl, ch, cl)
    part = (9 * mine, chans)
    give, dh, dl = call(
        functools.partial(give_kernel, total, scale),
        [part] + [bf(2, thin, wide)] * 2,
        flops=2 * work,
    )(*rows_of, fh, fl, gh, gl, pre, back)
    given = swapped(give, "core", 1)
    (keep,) = call(
        functools.partial(keep_kernel, total, scale), [part], flops=work
    )(*rows_of, dh, dl)
    whole = keep + given
    slices = lax.all_to_all(
        whole.reshape(n_image, slot, chans), ("pair", "half"), 0, 0, tiled=True
    )
    (gram,) = call(gram_kernel, [(1, 128)])(slices)
    sums = jnp.broadcast_to(gram, (n_image * n_band, gram.shape[1]))
    sums = lax.all_to_all(sums, AXES, 0, 0, tiled=True)
    (merged,) = call(functools.partial(merge_kernel, n_band), [(slot, chans)])(
        sums, slices
    )
    pieces = [merged] + [swapped(merged, "pair", k) for k in range(1, n_pair)]
    (block,) = call(gather_kernel, [(n_pair * slot, chans)])(*pieces)
    own = [block] + [swapped(block, ("half", "lo"), k) for k in range(1, n_band)]
    others = [swapped(piece, "core", 1) for piece in own]
    fresh = []
    for swap, blocks in enumerate((own, others)):
        fresh = [
            pl.pallas_call(
                functools.partial(final_kernel, n_pair, n_lo, swap),
                out_shape=jax.ShapeDtypeStruct((1,) + filters.shape, F32),
                in_specs=[pl.BlockSpec(memory_space=pltpu.SMEM)]
                + [pl.BlockSpec(memory_space=pltpu.VMEM)] * (1 + n_band)
                + [pl.BlockSpec(memory_space=pl.ANY)] * swap,
                out_specs=pl.BlockSpec(memory_space=pl.ANY),
                scratch_shapes=[
                    pltpu.VMEM((n_lo,) + part, F32),
                    pltpu.VMEM((kdim, chans), F32),
                    pltpu.SemaphoreType.DMA,
                ],
                input_output_aliases={2 + n_band: 0} if swap else {},
                compiler_params=pltpu.CompilerParams(vmem_limit_bytes=40 * 2**20),
            )(rates, filters, *blocks, *fresh)
        ]
    return fresh[0]


def with_rims(field):
    count = lax.axis_size("band")
    forward = [(i, i + 1) for i in range(count - 1)]
    backward = [(target, source) for source, target in forward]
    low = lax.ppermute(field[:, -1:], "band", forward)
    high = lax.ppermute(field[:, :1], "band", backward)
    extended = jnp.concatenate([low, field, high], axis=1)
    return jnp.pad(extended, ((0, 0), (0, 0), (1, 1)))


def taps(padded, rows, cols, flip=False):
    chans = padded.shape[0]
    at = (2, 1, 0) if flip else (0, 1, 2)
    pieces = [padded[:, dr : dr + rows, dc : dc + cols] for dr in at for dc in at]
    return jnp.stack(pieces, axis=1).reshape(chans, 9, rows * cols)


def plain(images, cotangent, filters, rates):
    feats, cot = images[0], cotangent[0]
    chans, rows, cols = feats.shape
    scale = (9 * chans) ** (-0.5)
    patch_one = taps(with_rims(feats), rows, cols).reshape(9 * chans, rows * cols)
    pre = scale * jnp.einsum("kc,kp->cp", filters[0], patch_one, precision=HIGH)
    hidden = jax.nn.silu(pre).reshape(chans, rows, cols)
    patch_two = taps(with_rims(hidden), rows, cols).reshape(9 * chans, rows * cols)
    back = taps(with_rims(cot), rows, cols, flip=True)
    flat_cot = cot.reshape(chans, rows * cols)
    grad_two = scale * jnp.einsum("kp,cp->kc", patch_two, flat_cot, precision=HIGH)
    weight_two = filters[1].reshape(chans, 9, chans)
    dhidden = scale * jnp.einsum("itc,ctp->ip", weight_two, back, precision=HIGH)
    sig = jax.nn.sigmoid(pre)
    dpre = dhidden * sig * (1.0 + pre * (1.0 - sig))
    grad_one = scale * jnp.einsum("kp,cp->kc", patch_one, dpre, precision=HIGH)
    block = lax.psum_scatter(
        jnp.stack([grad_one, grad_two]), "band", scatter_dimension=1, tiled=True
    )
    count = lax.axis_size("image")
    for level in range(count.bit_length() - 1):
        other = lax.ppermute(block, "image", xor_route(count, 1 << level))
        inner, own_sq, other_sq = lax.psum(
            tuple(jnp.sum(v, axis=(1, 2)) for v in (block * other, block * block, other * other)),
            "band",
        )
        low = (1.0 - inner / (2.0 * (own_sq + 1e-06)))[:, None, None]
        high = (1.0 - inner / (2.0 * (other_sq + 1e-06)))[:, None, None]
        block = low * block + high * other
    height = block.shape[1]
    mine = lax.dynamic_slice_in_dim(filters, lax.axis_index("band") * height, height, 1)
    fresh = (mine - rates[:, None, None] * block)[None]
    return lax.all_gather(fresh, "band", axis=2, tiled=True)


def power_of_two(n):
    return n & (n - 1) == 0


def solution(mesh):
    n_image, n_band = mesh.shape["image"], mesh.shape["band"]

    def step(images, cotangent, filters, rates):
        chans = images.shape[1]
        if (
            4 <= n_image
            and n_image**2 <= 128
            and 4 <= n_band
            and power_of_two(n_image)
            and power_of_two(n_band)
            and (9 * chans) % (n_band // 2 * n_image * 8) == 0
        ):
            shape = (n_image // 2, 2, 2, n_band // 2)
            split = jax.sharding.Mesh(mesh.devices.reshape(shape), AXES)
            image, band = ("pair", "core"), ("half", "lo")

            def body(*args):
                return fast(*args)

        else:
            split, image, band, body = mesh, "image", "band", plain
        whole = jax.shard_map(
            body,
            mesh=split,
            in_specs=(P(image, None, band, None), P(image, None, band, None), P(), P()),
            out_specs=P(image, None, None, None),
            check_vma=False,
        )
        return whole(images, cotangent, filters, rates)

    return step
```

```python
import functools

import jax
import jax.numpy as jnp
from jax import lax
from jax.experimental import pallas as pl
from jax.experimental.pallas import tpu as pltpu
from jax.sharding import PartitionSpec as P


HIGH = lax.Precision.HIGHEST
F32 = jnp.float32
BF16 = jnp.bfloat16


AXES = ("pair", "core", "half", "lo")


def call(body, outs, scratch=(), flops=0):
    outs = [o if isinstance(o, jax.ShapeDtypeStruct) else jax.ShapeDtypeStruct(o, F32) for o in outs]
    return pl.pallas_call(
        body,
        out_shape=outs,
        scratch_shapes=list(scratch),
        cost_estimate=pl.CostEstimate(flops=flops, bytes_accessed=flops // 500, transcendentals=0),
        compiler_params=pltpu.CompilerParams(vmem_limit_bytes=40 * 2**20),
    )


def halves(value):
    high = value.astype(BF16)
    return high, (value - high.astype(F32)).astype(BF16)


def dot3(ah, al, bh, bl, dims):
    def one(a, b):
        return lax.dot_general(a, b, (dims, ((), ())), preferred_element_type=F32)

    return one(ah, bh) + (one(ah, bl) + one(al, bh))


def moved(value, step):
    cols = value.shape[-1]
    col = lax.broadcasted_iota(jnp.int32, value.shape, value.ndim - 1)
    if step > 0:
        return jnp.where(col == cols - 1, 0.0, pltpu.roll(value, cols - 1, 1))
    return jnp.where(col == 0, 0.0, pltpu.roll(value, 1, 1))


def put(high_ref, low_ref, at, row, value):
    high, low = halves(value)
    rows, cols = value.shape
    part = (slice(at * rows, (at + 1) * rows), slice(row * cols, (row + 1) * cols))
    high_ref[part] = high
    low_ref[part] = low


def filter_kernel(f_ref, fh, fl, gh, gl, taps_ref):
    lo = lax.axis_index("lo")
    chans = f_ref.shape[2]
    mine = fh.shape[0] // 3
    rows = pl.ds(pl.multiple_of(lo * mine, 8), mine)
    for a in range(3):
        for b in range(3):
            t = 3 * a + b
            at = pl.ds(t, chans, stride=9)
            taps_ref[0, t] = f_ref[0, at, :].T
            taps_ref[1, t] = f_ref[1, at, :]
            put(fh, fl, b, a, taps_ref[0, t, rows, :])
            put(gh, gl, b, a, taps_ref[1, t, rows, :])


def sources(own, near, far):
    core, half, lo = (lax.axis_index(name) for name in ("core", "half", "lo"))
    kept = core == half
    return (
        (kept, own, lo),
        (kept, near, 1 - lo),
        (jnp.logical_not(kept), near, lo),
        (jnp.logical_not(kept), far, 1 - lo),
    )


def edge_kernel(own_ref, near_ref, far_ref, out):
    core = lax.axis_index("core")
    chans = out.shape[0]
    rows = own_ref.shape[0] // chans
    for wanted, ref, block in sources(own_ref, near_ref, far_ref):
        for c, row in ((0, rows - 1), (1, 0)):

            @pl.when(wanted & (core == c) & (block == 1 - c))
            def _():
                out[...] = ref[pl.ds(row, chans, stride=rows), :]


def rows_kernel(flip, own_ref, near_ref, far_ref, fh, fl, vh, vl, out, raw):
    total, chans, cols = raw.shape
    rows = own_ref.shape[0] // chans
    for wanted, ref, block in sources(own_ref, near_ref, far_ref):

        @pl.when(wanted)
        def _():
            for row in range(rows):
                raw[block * rows + row] = ref[pl.ds(row, chans, stride=rows), :]

    for a in range(3):
        step = 1 - a if flip else a - 1
        for row in range(total):
            value = raw[row + step] if 0 <= row + step < total else jnp.zeros((chans, cols), F32)
            put(vh, vl, a, row, value)
    out[...] = dot3(fh[...], fl[...], vh[...], vl[...], ((1,), (0,)))


def rims(edge, first, final, last):
    core = lax.axis_index("core")
    before = halves(jnp.where(core == 1, edge[...], 0.0))
    after = halves(jnp.where(core == 0, edge[...], 0.0))
    return {first: (0, before), final: (last, after)}


def layer_grad(out, scale, dh, dl, vh, vl, rim_of):
    mine = dh.shape[0] // 3
    chans, cols = rim_of[0][1][0].shape
    grad = dot3(dh[...], dl[...], vh[...], vl[...], ((1,), (1,)))
    for a in range(3):
        part = grad[:, a * chans : (a + 1) * chans]
        if a in rim_of:
            row, rim = rim_of[a]
            wide = slice(row * cols, (row + 1) * cols)
            part = part + dot3(dh[:, wide], dl[:, wide], *rim, ((1,), (1,)))
        for b in range(3):
            t = 3 * a + b
            out[t * mine : (t + 1) * mine, :] = scale * part[b * mine : (b + 1) * mine, :]


def row_sums(scale, wh, wl, ref, rim_of, total, flip):
    mine = wh.shape[0] // 3
    chans, cols = rim_of[0][1][0].shape
    rim_row = {
        row: dot3(
            wh[:, a * chans : (a + 1) * chans],
            wl[:, a * chans : (a + 1) * chans],
            *rim,
            ((1,), (0,)),
        )
        for a, (row, rim) in rim_of.items()
    }
    side = 1 if flip else -1
    found = []
    for row in range(total):
        wide = slice(row * cols, (row + 1) * cols)
        parts = []
        for b in range(3):
            value = ref[b * mine : (b + 1) * mine, wide]
            if row in rim_row:
                value = value + rim_row[row][b * mine : (b + 1) * mine, :]
            parts.append(value)
        found.append(scale * (parts[1] + moved(parts[0], side) + moved(parts[2], -side)))
    return found


def hidden_kernel(total, scale, edge, fh, fl, pre_ref, hh, hl, slope_ref):
    cols = edge.shape[1]
    for row, pre in enumerate(
        row_sums(scale, fh, fl, pre_ref, rims(edge, 0, 2, total - 1), total, False)
    ):
        sig = jax.nn.sigmoid(pre)
        hidden = pre * sig
        slope_ref[:, row * cols : (row + 1) * cols] = sig * (1.0 + pre * (1.0 - sig))
        for b, value in enumerate((moved(hidden, -1), hidden, moved(hidden, 1))):
            put(hh, hl, b, row, value)


def either(wanted, scale, out, x_edge, c_edge, xh, xl, ch, cl, hh, hl, dh, dl, last):

    @pl.when(wanted == 0)
    def _():
        layer_grad(out, scale, dh, dl, xh, xl, rims(x_edge, 0, 2, last))

    @pl.when(wanted == 1)
    def _():
        layer_grad(out, scale, hh, hl, ch, cl, rims(c_edge, 2, 0, last))


def give_kernel(total, scale, *refs):
    x_edge, c_edge, xh, xl, ch, cl, hh, hl, slope_ref, gh, gl, back_ref = refs[:12]
    give_ref, dh, dl = refs[12:]
    cols = x_edge.shape[1]
    for row, dhidden in enumerate(
        row_sums(scale, gh, gl, back_ref, rims(c_edge, 2, 0, total - 1), total, True)
    ):
        dpre = dhidden * slope_ref[:, row * cols : (row + 1) * cols]
        for b, value in enumerate((moved(dpre, 1), dpre, moved(dpre, -1))):
            put(dh, dl, b, row, value)
    wanted = 1 - lax.axis_index("core")
    either(wanted, scale, give_ref, x_edge, c_edge, xh, xl, ch, cl, hh, hl, dh, dl, total - 1)


def keep_kernel(total, scale, *refs):
    x_edge, c_edge, xh, xl, ch, cl, hh, hl, dh, dl, keep_ref = refs
    wanted = lax.axis_index("core")
    either(wanted, scale, keep_ref, x_edge, c_edge, xh, xl, ch, cl, hh, hl, dh, dl, total - 1)


def gram_kernel(v_ref, out):
    count = v_ref.shape[0]
    col = lax.broadcasted_iota(jnp.int32, out.shape, 1)
    total = jnp.zeros(out.shape, F32)
    for i in range(count):
        for j in range(i, count):
            value = jnp.sum(v_ref[i] * v_ref[j], keepdims=True)
            total = jnp.where((col == i * count + j) | (col == j * count + i), value, total)
    out[...] = total


def merge_kernel(n_band, sums_ref, v_ref, out):
    core = lax.axis_index("core")
    count = v_ref.shape[0]
    sums = sums_ref[...]
    lanes = sums.shape[1]
    device = lax.broadcasted_iota(jnp.int32, sums.shape, 0)
    same = ((device // n_band) % 2) == core
    flat = jnp.sum(jnp.where(same, sums, 0.0), 0, keepdims=True)
    row = lax.broadcasted_iota(jnp.int32, (count, lanes), 0)
    col = lax.broadcasted_iota(jnp.int32, (count, lanes), 1)
    gram = jnp.broadcast_to(flat, (count, lanes))
    wide = gram
    for i in range(1, count):
        gram = jnp.where(row == i, pltpu.roll(wide, lanes - i * count, 1), gram)
    gram = jnp.where(col < count, gram, 0.0)

    def swap(value, axis, step):
        size = value.shape[axis]
        index = row if axis == 0 else col
        return jnp.where(
            (index & step) != 0,
            pltpu.roll(value, step, axis),
            pltpu.roll(value, size - step, axis),
        )

    weight = jnp.ones((count, 1), F32)
    step = 1
    while step < count:
        own = jnp.where(row == col, gram, 0.0)
        cross = jnp.where((row ^ step) == col, gram, 0.0)
        down = 1.0 - jnp.sum(cross, 1, keepdims=True) / (
            2.0 * (jnp.sum(own, 1, keepdims=True) + 1e-06)
        )
        along = 1.0 - jnp.sum(cross, 0, keepdims=True) / (
            2.0 * (jnp.sum(own, 0, keepdims=True) + 1e-06)
        )
        weight = weight * down
        gram = gram * down * along
        gram = gram + swap(gram, 0, step)
        gram = gram + swap(gram, 1, step)
        step *= 2
    total = jnp.zeros(out.shape, F32)
    for i in range(count):
        total = total + weight[i : i + 1, :] * v_ref[i]
    out[...] = total


def gather_kernel(*refs):
    parts, out = refs[:-1], refs[-1]
    pair = lax.axis_index("pair")
    size = parts[0].shape[0]
    for k, part in enumerate(parts):
        start = pl.multiple_of(lax.bitwise_xor(pair, k) * size, 8)
        out[pl.ds(start, size), :] = part[...]


def new_layer(n_pair, n_lo, layer, rates_ref, f_ref, pieces, held, fresh):
    band = lax.axis_index("half") * n_lo + lax.axis_index("lo")
    size = pieces[0].shape[0] // n_pair
    chans = f_ref.shape[2]
    mine = chans // n_lo
    for k, piece in enumerate(pieces):
        place = lax.bitwise_xor(band, k)
        half, lo = place // n_lo, place % n_lo
        for p in range(n_pair):
            to = pl.ds(pl.multiple_of((2 * p + half) * size, 8), size)
            held[lo, to, :] = piece[p * size : (p + 1) * size, :]
    for l in range(2):

        @pl.when(layer == l)
        def _():
            rate = rates_ref[l]
            for t in range(9):
                at = pl.ds(t, chans, stride=9)
                value = held[:, t * mine : (t + 1) * mine, :].reshape(chans, chans)
                if l == 0:
                    value = value.T
                fresh[at, :] = f_ref[l, at, :] - rate * value


def own_kernel(n_pair, n_lo, rates_ref, f_ref, *refs):
    pieces, (fresh, held) = refs[:-2], refs[-2:]
    new_layer(n_pair, n_lo, lax.axis_index("core"), rates_ref, f_ref, pieces, held, fresh)


def final_kernel(n_pair, n_lo, rates_ref, f_ref, mine_ref, *refs):
    pieces, (out, held, fresh, sems) = refs[:-4], refs[-4:]
    core = lax.axis_index("core")
    first = pltpu.make_async_copy(mine_ref, out.at[0, core], sems.at[0])
    first.start()
    new_layer(n_pair, n_lo, 1 - core, rates_ref, f_ref, pieces, held, fresh)
    second = pltpu.make_async_copy(fresh, out.at[0, 1 - core], sems.at[1])
    second.start()
    first.wait()
    second.wait()


def xor_route(count, k):
    return [(i, i ^ k) for i in range(count)]


def swapped(value, axis, k):
    return lax.ppermute(value, axis, xor_route(lax.axis_size(axis), k))


def routes():
    def at(core, half, lo):
        return (core * 2 + half) * 2 + lo

    every = [(core, half, lo) for core in range(2) for half in range(2) for lo in range(2)]
    near = [(at(c, h, l), at(h, c, 1 - l if c == h else l)) for c, h, l in every]
    far = [(at(c, h, l), at(h, c, 1 - l)) for c, h, l in every if c != h]
    onward = [(at(c, h, l), at(c, h, 1 - l)) for c, h, l in every if c != h]
    return near, far, onward


def sent(value, route):
    return lax.ppermute(value, ("core", "half", "lo"), route)


def fast(images, cotangent, filters, rates):
    _, chans, rows, cols = images.shape
    n_pair, n_lo = lax.axis_size("pair"), lax.axis_size("lo")
    n_image, n_band = 2 * n_pair, 2 * n_lo
    kdim = filters.shape[1]
    mine = chans // n_lo
    total = n_lo * rows
    slot = 9 * mine // n_image
    flat = (chans * rows, cols)
    bf = lambda *shape: jax.ShapeDtypeStruct(shape, BF16)
    tall, thin, wide = 3 * chans, 3 * mine, total * cols
    near, far, onward = routes()
    c_near = sent(cotangent, near)
    x_near = sent(images, near)
    x_far = sent(images, far)
    c_far = sent(c_near, onward)
    xs = [v.reshape(flat) for v in (images, x_near, x_far)]
    cs = [v.reshape(flat) for v in (cotangent, c_near, c_far)]
    fh, fl, gh, gl = call(
        filter_kernel, [bf(thin, tall)] * 4, [pltpu.VMEM((2, 9, chans, chans), F32)]
    )(filters)
    (edge,) = call(edge_kernel, [(chans, cols)])(*xs)
    x_edge = swapped(edge, "core", 1)
    raw = [pltpu.VMEM((total, chans, cols), F32)]
    work = 6 * thin * tall * wide
    outs = [bf(tall, wide)] * 2 + [(thin, wide)]
    xh, xl, pre = call(functools.partial(rows_kernel, False), outs, raw, flops=work)(*xs, fh, fl)
    scale = kdim ** (-0.5)
    hh, hl, slope = call(
        functools.partial(hidden_kernel, total, scale), [bf(thin, wide)] * 2 + [(mine, wide)]
    )(x_edge, fh, fl, pre)
    (edge,) = call(edge_kernel, [(chans, cols)])(*cs)
    c_edge = swapped(edge, "core", 1)
    ch, cl, back = call(functools.partial(rows_kernel, True), outs, raw, flops=work)(*cs, gh, gl)
    rows_of = (x_edge, c_edge, xh, xl, ch, cl, hh, hl)
    part = (9 * mine, chans)
    give, dh, dl = call(
        functools.partial(give_kernel, total, scale), [part] + [bf(thin, wide)] * 2, flops=2 * work
    )(*rows_of, slope, gh, gl, back)
    given = swapped(give, "core", 1)
    (keep,) = call(
        functools.partial(keep_kernel, total, scale), [part], flops=work
    )(*rows_of, dh, dl)
    whole = keep + given
    slices = lax.all_to_all(
        whole.reshape(n_image, slot, chans), ("pair", "half"), 0, 0, tiled=True
    )
    (gram,) = call(gram_kernel, [(1, 128)])(slices)
    sums = jnp.broadcast_to(gram, (n_image * n_band, gram.shape[1]))
    sums = lax.all_to_all(sums, AXES, 0, 0, tiled=True)
    (merged,) = call(functools.partial(merge_kernel, n_band), [(slot, chans)])(sums, slices)
    pieces = [merged] + [swapped(merged, "pair", k) for k in range(1, n_pair)]
    (block,) = call(gather_kernel, [(n_pair * slot, chans)])(*pieces)
    own = [block] + [swapped(block, ("half", "lo"), k) for k in range(1, n_band)]
    others = [swapped(piece, "core", 1) for piece in own]
    layer = (kdim, chans)
    held = pltpu.VMEM((n_lo,) + part, F32)
    vmem, smem = (pl.BlockSpec(memory_space=m) for m in (pltpu.VMEM, pltpu.SMEM))
    params = pltpu.CompilerParams(vmem_limit_bytes=40 * 2**20)
    fresh = pl.pallas_call(
        functools.partial(own_kernel, n_pair, n_lo),
        out_shape=jax.ShapeDtypeStruct(layer, F32),
        in_specs=[smem] + [vmem] * (1 + n_band),
        out_specs=vmem,
        scratch_shapes=[held],
        compiler_params=params,
    )(rates, filters, *own)
    return pl.pallas_call(
        functools.partial(final_kernel, n_pair, n_lo),
        out_shape=jax.ShapeDtypeStruct((1,) + filters.shape, F32),
        in_specs=[smem] + [vmem] * (2 + n_band),
        out_specs=pl.BlockSpec(memory_space=pl.ANY),
        scratch_shapes=[held, pltpu.VMEM(layer, F32), pltpu.SemaphoreType.DMA((2,))],
        compiler_params=params,
    )(rates, filters, fresh, *others)


def with_rims(field):
    count = lax.axis_size("band")
    forward = [(i, i + 1) for i in range(count - 1)]
    backward = [(target, source) for source, target in forward]
    low = lax.ppermute(field[:, -1:], "band", forward)
    high = lax.ppermute(field[:, :1], "band", backward)
    extended = jnp.concatenate([low, field, high], axis=1)
    return jnp.pad(extended, ((0, 0), (0, 0), (1, 1)))


def taps(padded, rows, cols, flip=False):
    chans = padded.shape[0]
    at = (2, 1, 0) if flip else (0, 1, 2)
    pieces = [padded[:, dr : dr + rows, dc : dc + cols] for dr in at for dc in at]
    return jnp.stack(pieces, axis=1).reshape(chans, 9, rows * cols)


def plain(images, cotangent, filters, rates):
    feats, cot = images[0], cotangent[0]
    chans, rows, cols = feats.shape
    scale = (9 * chans) ** (-0.5)
    patch_one = taps(with_rims(feats), rows, cols).reshape(9 * chans, rows * cols)
    pre = scale * jnp.einsum("kc,kp->cp", filters[0], patch_one, precision=HIGH)
    hidden = jax.nn.silu(pre).reshape(chans, rows, cols)
    patch_two = taps(with_rims(hidden), rows, cols).reshape(9 * chans, rows * cols)
    back = taps(with_rims(cot), rows, cols, flip=True)
    flat_cot = cot.reshape(chans, rows * cols)
    grad_two = scale * jnp.einsum("kp,cp->kc", patch_two, flat_cot, precision=HIGH)
    weight_two = filters[1].reshape(chans, 9, chans)
    dhidden = scale * jnp.einsum("itc,ctp->ip", weight_two, back, precision=HIGH)
    sig = jax.nn.sigmoid(pre)
    dpre = dhidden * sig * (1.0 + pre * (1.0 - sig))
    grad_one = scale * jnp.einsum("kp,cp->kc", patch_one, dpre, precision=HIGH)
    block = lax.psum_scatter(
        jnp.stack([grad_one, grad_two]), "band", scatter_dimension=1, tiled=True
    )
    count = lax.axis_size("image")
    for level in range(count.bit_length() - 1):
        other = lax.ppermute(block, "image", xor_route(count, 1 << level))
        inner, own_sq, other_sq = lax.psum(
            tuple(jnp.sum(v, axis=(1, 2)) for v in (block * other, block * block, other * other)),
            "band",
        )
        low = (1.0 - inner / (2.0 * (own_sq + 1e-06)))[:, None, None]
        high = (1.0 - inner / (2.0 * (other_sq + 1e-06)))[:, None, None]
        block = low * block + high * other
    height = block.shape[1]
    mine = lax.dynamic_slice_in_dim(filters, lax.axis_index("band") * height, height, 1)
    fresh = (mine - rates[:, None, None] * block)[None]
    return lax.all_gather(fresh, "band", axis=2, tiled=True)


def power_of_two(n):
    return n & (n - 1) == 0


def solution(mesh):
    n_image, n_band = mesh.shape["image"], mesh.shape["band"]

    def step(images, cotangent, filters, rates):
        chans = images.shape[1]
        if (
            4 <= n_image
            and n_image**2 <= 128
            and n_band == 4
            and power_of_two(n_image)
            and (9 * chans) % (n_band // 2 * n_image * 8) == 0
        ):
            shape = (n_image // 2, 2, 2, n_band // 2)
            split = jax.sharding.Mesh(mesh.devices.reshape(shape), AXES)
            image, band = ("pair", "core"), ("half", "lo")

            def body(*args):
                return fast(*args)

        else:
            split, image, band, body = mesh, "image", "band", plain
        whole = jax.shard_map(
            body,
            mesh=split,
            in_specs=(P(image, None, band, None), P(image, None, band, None), P(), P()),
            out_specs=P(image, None, None, None),
            check_vma=False,
        )
        return whole(images, cotangent, filters, rates)

    return step
```

```python
import functools

import jax
import jax.numpy as jnp
from jax import lax
from jax.experimental import pallas as pl
from jax.experimental.pallas import tpu as pltpu
from jax.sharding import PartitionSpec as P


HIGH = lax.Precision.HIGHEST
F32 = jnp.float32
BF16 = jnp.bfloat16


AXES = ("pair", "core", "half", "lo")


def call(body, outs, scratch=(), flops=0):
    outs = [o if isinstance(o, jax.ShapeDtypeStruct) else jax.ShapeDtypeStruct(o, F32) for o in outs]
    return pl.pallas_call(
        body,
        out_shape=outs,
        scratch_shapes=list(scratch),
        cost_estimate=pl.CostEstimate(flops=flops, bytes_accessed=flops // 500, transcendentals=0),
        compiler_params=pltpu.CompilerParams(vmem_limit_bytes=40 * 2**20),
    )


def halves(value):
    high = value.astype(BF16)
    return high, (value - high.astype(F32)).astype(BF16)


def product(a, b, dims=((1,), (0,))):
    return lax.dot_general(a, b, (dims, ((), ())), preferred_element_type=F32)


def dot3(ah, al, bh, bl, dims):
    return product(ah, bh, dims) + (product(ah, bl, dims) + product(al, bh, dims))


def moved(value, step):
    cols = value.shape[-1]
    col = lax.broadcasted_iota(jnp.int32, value.shape, value.ndim - 1)
    if step > 0:
        return jnp.where(col == cols - 1, 0.0, pltpu.roll(value, cols - 1, 1))
    return jnp.where(col == 0, 0.0, pltpu.roll(value, 1, 1))


def put(high_ref, low_ref, at, row, value):
    high, low = halves(value)
    rows, cols = value.shape
    part = (slice(at * rows, (at + 1) * rows), slice(row * cols, (row + 1) * cols))
    high_ref[part] = high
    low_ref[part] = low


def filter_kernel(f_ref, x_ref, c_ref, fh, fl, gh, gl, x_out, c_out, taps_ref):
    x_out[...] = x_ref[...]
    c_out[...] = c_ref[...]
    lo = lax.axis_index("lo")
    chans = f_ref.shape[2]
    mine = fh.shape[0] // 3
    rows = pl.ds(pl.multiple_of(lo * mine, 8), mine)
    for a in range(3):
        for b in range(3):
            t = 3 * a + b
            at = pl.ds(t, chans, stride=9)
            taps_ref[0, t] = f_ref[0, at, :].T
            taps_ref[1, t] = f_ref[1, at, :]
            to = slice(b * mine, (b + 1) * mine)
            for layer, wh, wl in ((0, fh, fl), (1, gh, gl)):
                high, low = halves(taps_ref[layer, t, rows, :])
                wh[to, a * chans : (a + 1) * chans] = high
                wh[to, (3 + a) * chans : (4 + a) * chans] = high
                wl[to, a * chans : (a + 1) * chans] = low


def sources(own, near, far):
    core, half, lo = (lax.axis_index(name) for name in ("core", "half", "lo"))
    kept = core == half
    return (
        (kept, own, lo),
        (kept, near, 1 - lo),
        (jnp.logical_not(kept), near, lo),
        (jnp.logical_not(kept), far, 1 - lo),
    )


def edge_kernel(own_ref, near_ref, far_ref, out):
    core = lax.axis_index("core")
    chans = out.shape[0]
    rows = own_ref.shape[0] // chans
    for wanted, ref, block in sources(own_ref, near_ref, far_ref):
        for c, row in ((0, rows - 1), (1, 0)):

            @pl.when(wanted & (core == c) & (block == 1 - c))
            def _():
                out[...] = ref[pl.ds(row, chans, stride=rows), :]


def side_kernel(near_ref, far_ref, out):
    core, lo = lax.axis_index("core"), lax.axis_index("lo")
    chans = out.shape[0]
    rows = near_ref.shape[0] // chans
    for ref, block in ((near_ref, lo), (far_ref, 1 - lo)):
        for c, row in ((0, rows - 1), (1, 0)):

            @pl.when((core == c) & (block == 1 - c))
            def _():
                out[...] = ref[pl.ds(row, chans, stride=rows), :]


def rows_kernel(flip, own_ref, near_ref, far_ref, fh, fl, v_ref, out, raw):
    total, chans, cols = raw.shape
    rows = own_ref.shape[0] // chans
    for wanted, ref, block in sources(own_ref, near_ref, far_ref):

        @pl.when(wanted)
        def _():
            for row in range(rows):
                raw[block * rows + row] = ref[pl.ds(row, chans, stride=rows), :]

    for row in range(-1, total + 1):
        inside = 0 <= row < total
        high, low = halves(raw[row] if inside else jnp.zeros((chans, cols), F32))
        for a in range(3):
            to = row + a - 1 if flip else row - a + 1
            if 0 <= to < total:
                wide = slice(to * cols, (to + 1) * cols)
                v_ref[a * chans : (a + 1) * chans, wide] = high
                v_ref[(3 + a) * chans : (4 + a) * chans, wide] = low
    out[...] = product(fh[...], v_ref[...]) + product(fl[...], v_ref[: 3 * chans, :])


def rims(edge, first, final, last):
    core = lax.axis_index("core")
    before = halves(jnp.where(core == 1, edge, 0.0))
    after = halves(jnp.where(core == 0, edge, 0.0))
    return {first: (0, before), final: (last, after)}


def layer_grad(out, scale, taps, dh, dl, v_ref, rim_of):
    chans, cols = rim_of[0][1][0].shape
    low = v_ref.shape[0] // 2
    nt = ((1,), (1,))
    first, size = taps[0] * chans, len(taps) * chans
    high_rows = v_ref[first : first + size, :]
    low_rows = v_ref[low + first : low + first + size, :]
    grad = dot3(high_rows, low_rows, dh[...], dl[...], nt)
    for at, a in enumerate(taps):
        part = grad[at * chans : (at + 1) * chans, :]
        if a in rim_of:
            row, rim = rim_of[a]
            wide = slice(row * cols, (row + 1) * cols)
            part = part + dot3(*rim, dh[:, wide], dl[:, wide], nt)
        thin = part.shape[1]
        out[at * thin : (at + 1) * thin, :] = scale * part.T


def either(wanted, scale, taps, out, x_edge, c_edge, xv, cv, hh, hl, dh, dl, last):
    @pl.when(wanted == 0)
    def _():
        layer_grad(out, scale, taps, dh, dl, xv, rims(x_edge[...], 0, 2, last))

    @pl.when(wanted == 1)
    def _():
        layer_grad(out, scale, taps, hh, hl, cv, rims(c_edge, 2, 0, last))


def one_of(early_ref, late_ref):
    kept = lax.axis_index("core") == lax.axis_index("half")
    return jnp.where(kept, late_ref[...], early_ref[...])


def row_sums(scale, wh, wl, ref, rim_of, total, flip):
    mine = wh.shape[0] // 3
    chans, cols = rim_of[0][1][0].shape
    rim_row = {
        row: dot3(
            wh[:, a * chans : (a + 1) * chans],
            wl[:, a * chans : (a + 1) * chans],
            *rim,
            ((1,), (0,)),
        )
        for a, (row, rim) in rim_of.items()
    }
    side = 1 if flip else -1
    found = []
    for row in range(total):
        wide = slice(row * cols, (row + 1) * cols)
        parts = []
        for b in range(3):
            value = ref[b * mine : (b + 1) * mine, wide]
            if row in rim_row:
                value = value + rim_row[row][b * mine : (b + 1) * mine, :]
            parts.append(value)
        found.append(scale * (parts[1] + moved(parts[0], side) + moved(parts[2], -side)))
    return found


def hidden_kernel(total, scale, edge, fh, fl, pre_ref, hh, hl, slope_ref):
    cols = edge.shape[1]
    for row, pre in enumerate(
        row_sums(scale, fh, fl, pre_ref, rims(edge[...], 0, 2, total - 1), total, False)
    ):
        sig = jax.nn.sigmoid(pre)
        hidden = pre * sig
        slope_ref[:, row * cols : (row + 1) * cols] = sig * (1.0 + pre * (1.0 - sig))
        for b, value in enumerate((moved(hidden, -1), hidden, moved(hidden, 1))):
            put(hh, hl, b, row, value)


def first_kernel(total, scale, taps, *refs):
    x_edge, early, late, xv, cv, hh, hl, slope_ref, gh, gl, back_ref, give_ref, dh, dl = refs
    cols = x_edge.shape[1]
    c_edge = one_of(early, late)
    for row, dhidden in enumerate(
        row_sums(scale, gh, gl, back_ref, rims(c_edge, 2, 0, total - 1), total, True)
    ):
        dpre = dhidden * slope_ref[:, row * cols : (row + 1) * cols]
        for b, value in enumerate((moved(dpre, 1), dpre, moved(dpre, -1))):
            put(dh, dl, b, row, value)
    wanted = 1 - lax.axis_index("core")
    either(wanted, scale, taps, give_ref, x_edge, c_edge, xv, cv, hh, hl, dh, dl, total - 1)


def grad_kernel(total, scale, taps, give, *refs):
    x_edge, early, late, xv, cv, hh, hl, dh, dl, out = refs
    core = lax.axis_index("core")
    wanted = 1 - core if give else core
    c_edge = one_of(early, late)
    either(wanted, scale, taps, out, x_edge, c_edge, xv, cv, hh, hl, dh, dl, total - 1)


def gram_kernel(v_ref, out):
    count = v_ref.shape[0]
    col = lax.broadcasted_iota(jnp.int32, out.shape, 1)
    total = jnp.zeros(out.shape, F32)
    for i in range(count):
        for j in range(i, count):
            value = jnp.sum(v_ref[i] * v_ref[j], keepdims=True)
            total = jnp.where((col == i * count + j) | (col == j * count + i), value, total)
    out[...] = total


def merge_kernel(n_band, sums_ref, v_ref, out):
    core = lax.axis_index("core")
    count = v_ref.shape[0]
    sums = sums_ref[...]
    lanes = sums.shape[1]
    device = lax.broadcasted_iota(jnp.int32, sums.shape, 0)
    same = ((device // n_band) % 2) == core
    flat = jnp.sum(jnp.where(same, sums, 0.0), 0, keepdims=True)
    row = lax.broadcasted_iota(jnp.int32, (count, lanes), 0)
    col = lax.broadcasted_iota(jnp.int32, (count, lanes), 1)
    gram = jnp.broadcast_to(flat, (count, lanes))
    wide = gram
    for i in range(1, count):
        gram = jnp.where(row == i, pltpu.roll(wide, lanes - i * count, 1), gram)
    gram = jnp.where(col < count, gram, 0.0)

    def swap(value, axis, step):
        size = value.shape[axis]
        index = row if axis == 0 else col
        return jnp.where(
            (index & step) != 0,
            pltpu.roll(value, step, axis),
            pltpu.roll(value, size - step, axis),
        )

    weight = jnp.ones((count, 1), F32)
    step = 1
    while step < count:
        own = jnp.where(row == col, gram, 0.0)
        cross = jnp.where((row ^ step) == col, gram, 0.0)
        down = 1.0 - jnp.sum(cross, 1, keepdims=True) / (
            2.0 * (jnp.sum(own, 1, keepdims=True) + 1e-06)
        )
        along = 1.0 - jnp.sum(cross, 0, keepdims=True) / (
            2.0 * (jnp.sum(own, 0, keepdims=True) + 1e-06)
        )
        weight = weight * down
        gram = gram * down * along
        gram = gram + swap(gram, 0, step)
        gram = gram + swap(gram, 1, step)
        step *= 2
    total = jnp.zeros(out.shape, F32)
    for i in range(count):
        total = total + weight[i : i + 1, :] * v_ref[i]
    out[...] = total


def gather_kernel(*refs):
    parts, out = refs[:-1], refs[-1]
    pair = lax.axis_index("pair")
    size = parts[0].shape[0]
    for k, part in enumerate(parts):
        start = pl.multiple_of(lax.bitwise_xor(pair, k) * size, 8)
        out[pl.ds(start, size), :] = part[...]


def new_layer(n_pair, n_lo, layer, rates_ref, f_ref, pieces, held, fresh):
    band = lax.axis_index("half") * n_lo + lax.axis_index("lo")
    size = pieces[0].shape[0] // n_pair
    chans = f_ref.shape[2]
    mine = chans // n_lo
    for k, piece in enumerate(pieces):
        place = lax.bitwise_xor(band, k)
        half, lo = place // n_lo, place % n_lo
        for p in range(n_pair):
            to = pl.ds(pl.multiple_of((2 * p + half) * size, 8), size)
            held[lo, to, :] = piece[p * size : (p + 1) * size, :]
    for l in range(2):

        @pl.when(layer == l)
        def _():
            rate = rates_ref[l]
            for t in range(9):
                at = pl.ds(t, chans, stride=9)
                value = held[:, t * mine : (t + 1) * mine, :].reshape(chans, chans)
                if l == 0:
                    value = value.T
                fresh[at, :] = f_ref[l, at, :] - rate * value


def own_kernel(n_pair, n_lo, rates_ref, f_ref, *refs):
    pieces, (fresh, held) = refs[:-2], refs[-2:]
    new_layer(n_pair, n_lo, lax.axis_index("core"), rates_ref, f_ref, pieces, held, fresh)


def final_kernel(n_pair, n_lo, rates_ref, f_ref, mine_ref, *refs):
    pieces, (out, held, fresh, sems) = refs[:-4], refs[-4:]
    core = lax.axis_index("core")
    first = pltpu.make_async_copy(mine_ref, out.at[0, core], sems.at[0])
    first.start()
    new_layer(n_pair, n_lo, 1 - core, rates_ref, f_ref, pieces, held, fresh)
    second = pltpu.make_async_copy(fresh, out.at[0, 1 - core], sems.at[1])
    second.start()
    first.wait()
    second.wait()


def xor_route(count, k):
    return [(i, i ^ k) for i in range(count)]


def swapped(value, axis, k):
    return lax.ppermute(value, axis, xor_route(lax.axis_size(axis), k))


def routes():
    def at(core, half, lo):
        return (core * 2 + half) * 2 + lo

    every = [(core, half, lo) for core in range(2) for half in range(2) for lo in range(2)]
    near = [(at(c, h, l), at(h, c, 1 - l if c == h else l)) for c, h, l in every]
    far = [(at(c, h, l), at(h, c, 1 - l)) for c, h, l in every if c != h]
    onward = [(at(c, h, l), at(c, h, 1 - l)) for c, h, l in every if c != h]
    return near, far, onward


def rim_routes():
    every = [(core, half, lo) for core in range(2) for half in range(2) for lo in range(2)]
    pairs = [(c == h, ((c * 2 + h) * 2 + l, ((1 - c) * 2 + h) * 2 + l)) for c, h, l in every]
    return [[pair for kept, pair in pairs if kept == want] for want in (True, False)]


def sent(value, route):
    return lax.ppermute(value, ("core", "half", "lo"), route)


def fast(images, cotangent, filters, rates):
    _, chans, rows, cols = images.shape
    n_pair, n_lo = lax.axis_size("pair"), lax.axis_size("lo")
    n_image, n_band = 2 * n_pair, 2 * n_lo
    kdim = filters.shape[1]
    mine = chans // n_lo
    total = n_lo * rows
    slot = 9 * mine // n_image
    flat = (chans * rows, cols)
    bf = lambda *shape: jax.ShapeDtypeStruct(shape, BF16)
    tall, thin, wide = 3 * chans, 3 * mine, total * cols
    near, far, onward = routes()
    c_near = sent(cotangent, near)
    x_near = sent(images, near)
    x_far = sent(images, far)
    c_far = sent(c_near, onward)
    fh, fl, gh, gl, x_own, c_own = call(
        filter_kernel,
        [bf(thin, 2 * tall), bf(thin, tall)] * 2 + [flat, flat],
        [pltpu.VMEM((2, 9, chans, chans), F32)],
    )(filters, images.reshape(flat), cotangent.reshape(flat))
    xs = [x_own] + [v.reshape(flat) for v in (x_near, x_far)]
    cs = [c_own] + [v.reshape(flat) for v in (c_near, c_far)]
    (edge,) = call(edge_kernel, [(chans, cols)])(*xs)
    x_edge = swapped(edge, "core", 1)
    raw = [pltpu.VMEM((total, chans, cols), F32)]
    work = 6 * thin * tall * wide
    outs = [bf(2 * tall, wide), (thin, wide)]
    xv, pre = call(functools.partial(rows_kernel, False), outs, raw, flops=work)(*xs, fh, fl)
    scale = kdim ** (-0.5)
    hh, hl, slope = call(
        functools.partial(hidden_kernel, total, scale), [bf(thin, wide)] * 2 + [(mine, wide)]
    )(x_edge, fh, fl, pre)
    (edge,) = call(side_kernel, [(chans, cols)])(*cs[:2])
    early = sent(edge, rim_routes()[0])
    (edge,) = call(side_kernel, [(chans, cols)])(*cs[1:])
    late = sent(edge, rim_routes()[1])
    cv, back = call(functools.partial(rows_kernel, True), outs, raw, flops=work)(*cs, gh, gl)
    known = (x_edge, early, late, xv, cv, hh, hl)
    part = (9 * mine, chans)
    give, dh, dl = call(
        functools.partial(first_kernel, total, scale, (0, 1)),
        [(2 * thin, chans)] + [bf(thin, wide)] * 2,
        flops=work,
    )(*known, slope, gh, gl, back)
    given = [swapped(give, "core", 1)]
    (give,) = call(
        functools.partial(grad_kernel, total, scale, (2,), True), [(thin, chans)], flops=work // 3
    )(*known, dh, dl)
    given.append(swapped(give, "core", 1))
    (keep,) = call(
        functools.partial(grad_kernel, total, scale, (0, 1, 2), False), [part], flops=work
    )(*known, dh, dl)
    whole = keep + jnp.concatenate(given)
    slices = lax.all_to_all(
        whole.reshape(n_image, slot, chans), ("pair", "half"), 0, 0, tiled=True
    )
    (gram,) = call(gram_kernel, [(1, 128)])(slices)
    sums = jnp.broadcast_to(gram, (n_image * n_band, gram.shape[1]))
    sums = lax.all_to_all(sums, AXES, 0, 0, tiled=True)
    (merged,) = call(functools.partial(merge_kernel, n_band), [(slot, chans)])(sums, slices)
    pieces = [merged] + [swapped(merged, "pair", k) for k in range(1, n_pair)]
    (block,) = call(gather_kernel, [(n_pair * slot, chans)])(*pieces)
    own = [block] + [swapped(block, ("half", "lo"), k) for k in range(1, n_band)]
    others = [swapped(piece, "core", 1) for piece in own]
    layer = (kdim, chans)
    held = pltpu.VMEM((n_lo,) + part, F32)
    vmem, smem = (pl.BlockSpec(memory_space=m) for m in (pltpu.VMEM, pltpu.SMEM))
    params = pltpu.CompilerParams(vmem_limit_bytes=40 * 2**20)
    fresh = pl.pallas_call(
        functools.partial(own_kernel, n_pair, n_lo),
        out_shape=jax.ShapeDtypeStruct(layer, F32),
        in_specs=[smem] + [vmem] * (1 + n_band),
        out_specs=vmem,
        scratch_shapes=[held],
        compiler_params=params,
    )(rates, filters, *own)
    return pl.pallas_call(
        functools.partial(final_kernel, n_pair, n_lo),
        out_shape=jax.ShapeDtypeStruct((1,) + filters.shape, F32),
        in_specs=[smem] + [vmem] * (2 + n_band),
        out_specs=pl.BlockSpec(memory_space=pl.ANY),
        scratch_shapes=[held, pltpu.VMEM(layer, F32), pltpu.SemaphoreType.DMA((2,))],
        compiler_params=params,
    )(rates, filters, fresh, *others)


def with_rims(field):
    count = lax.axis_size("band")
    forward = [(i, i + 1) for i in range(count - 1)]
    backward = [(target, source) for source, target in forward]
    low = lax.ppermute(field[:, -1:], "band", forward)
    high = lax.ppermute(field[:, :1], "band", backward)
    extended = jnp.concatenate([low, field, high], axis=1)
    return jnp.pad(extended, ((0, 0), (0, 0), (1, 1)))


def taps(padded, rows, cols, flip=False):
    chans = padded.shape[0]
    at = (2, 1, 0) if flip else (0, 1, 2)
    pieces = [padded[:, dr : dr + rows, dc : dc + cols] for dr in at for dc in at]
    return jnp.stack(pieces, axis=1).reshape(chans, 9, rows * cols)


def plain(images, cotangent, filters, rates):
    feats, cot = images[0], cotangent[0]
    chans, rows, cols = feats.shape
    scale = (9 * chans) ** (-0.5)
    patch_one = taps(with_rims(feats), rows, cols).reshape(9 * chans, rows * cols)
    pre = scale * jnp.einsum("kc,kp->cp", filters[0], patch_one, precision=HIGH)
    hidden = jax.nn.silu(pre).reshape(chans, rows, cols)
    patch_two = taps(with_rims(hidden), rows, cols).reshape(9 * chans, rows * cols)
    back = taps(with_rims(cot), rows, cols, flip=True)
    flat_cot = cot.reshape(chans, rows * cols)
    grad_two = scale * jnp.einsum("kp,cp->kc", patch_two, flat_cot, precision=HIGH)
    weight_two = filters[1].reshape(chans, 9, chans)
    dhidden = scale * jnp.einsum("itc,ctp->ip", weight_two, back, precision=HIGH)
    sig = jax.nn.sigmoid(pre)
    dpre = dhidden * sig * (1.0 + pre * (1.0 - sig))
    grad_one = scale * jnp.einsum("kp,cp->kc", patch_one, dpre, precision=HIGH)
    block = lax.psum_scatter(
        jnp.stack([grad_one, grad_two]), "band", scatter_dimension=1, tiled=True
    )
    count = lax.axis_size("image")
    for level in range(count.bit_length() - 1):
        other = lax.ppermute(block, "image", xor_route(count, 1 << level))
        inner, own_sq, other_sq = lax.psum(
            tuple(jnp.sum(v, axis=(1, 2)) for v in (block * other, block * block, other * other)),
            "band",
        )
        low = (1.0 - inner / (2.0 * (own_sq + 1e-06)))[:, None, None]
        high = (1.0 - inner / (2.0 * (other_sq + 1e-06)))[:, None, None]
        block = low * block + high * other
    height = block.shape[1]
    mine = lax.dynamic_slice_in_dim(filters, lax.axis_index("band") * height, height, 1)
    fresh = (mine - rates[:, None, None] * block)[None]
    return lax.all_gather(fresh, "band", axis=2, tiled=True)


def power_of_two(n):
    return n & (n - 1) == 0


def solution(mesh):
    n_image, n_band = mesh.shape["image"], mesh.shape["band"]

    def step(images, cotangent, filters, rates):
        chans = images.shape[1]
        if (
            4 <= n_image
            and n_image**2 <= 128
            and n_band == 4
            and power_of_two(n_image)
            and (9 * chans) % (n_band // 2 * n_image * 8) == 0
        ):
            shape = (n_image // 2, 2, 2, n_band // 2)
            split = jax.sharding.Mesh(mesh.devices.reshape(shape), AXES)
            image, band = ("pair", "core"), ("half", "lo")

            def body(*args):
                return fast(*args)

        else:
            split, image, band, body = mesh, "image", "band", plain
        whole = jax.shard_map(
            body,
            mesh=split,
            in_specs=(P(image, None, band, None), P(image, None, band, None), P(), P()),
            out_specs=P(image, None, None, None),
            check_vma=False,
        )
        return whole(images, cotangent, filters, rates)

    return step
```

```python
import functools

import jax
import jax.numpy as jnp
from jax import lax
from jax.experimental import pallas as pl
from jax.experimental.pallas import tpu as pltpu
from jax.sharding import PartitionSpec as P


HIGH = lax.Precision.HIGHEST
F32 = jnp.float32
BF16 = jnp.bfloat16


AXES = ("pair", "core", "half", "lo")


def call(body, outs, scratch=(), flops=0):
    outs = [o if isinstance(o, jax.ShapeDtypeStruct) else jax.ShapeDtypeStruct(o, F32) for o in outs]
    return pl.pallas_call(
        body,
        out_shape=outs,
        scratch_shapes=list(scratch),
        cost_estimate=pl.CostEstimate(flops=flops, bytes_accessed=flops // 500, transcendentals=0),
        compiler_params=pltpu.CompilerParams(vmem_limit_bytes=40 * 2**20),
    )


def halves(value):
    high = value.astype(BF16)
    return high, (value - high.astype(F32)).astype(BF16)


def product(a, b, dims=((1,), (0,))):
    return lax.dot_general(a, b, (dims, ((), ())), preferred_element_type=F32)


def dot3(ah, al, bh, bl, dims):
    return product(ah, bh, dims) + (product(ah, bl, dims) + product(al, bh, dims))


def moved(value, step):
    cols = value.shape[-1]
    col = lax.broadcasted_iota(jnp.int32, value.shape, value.ndim - 1)
    if step > 0:
        return jnp.where(col == cols - 1, 0.0, pltpu.roll(value, cols - 1, 1))
    return jnp.where(col == 0, 0.0, pltpu.roll(value, 1, 1))


def put(high_ref, low_ref, at, row, value):
    high, low = halves(value)
    rows, cols = value.shape
    part = (slice(at * rows, (at + 1) * rows), slice(row * cols, (row + 1) * cols))
    high_ref[part] = high
    low_ref[part] = low


def filter_kernel(f_ref, fh, fl, gh, gl, taps_ref):
    lo = lax.axis_index("lo")
    chans = f_ref.shape[2]
    mine = fh.shape[0] // 3
    rows = pl.ds(pl.multiple_of(lo * mine, 8), mine)
    for a in range(3):
        for b in range(3):
            t = 3 * a + b
            at = pl.ds(t, chans, stride=9)
            taps_ref[0, t] = f_ref[0, at, :].T
            taps_ref[1, t] = f_ref[1, at, :]
            to = slice(b * mine, (b + 1) * mine)
            for layer, wh, wl in ((0, fh, fl), (1, gh, gl)):
                high, low = halves(taps_ref[layer, t, rows, :])
                wh[to, a * chans : (a + 1) * chans] = high
                wh[to, (3 + a) * chans : (4 + a) * chans] = high
                wl[to, a * chans : (a + 1) * chans] = low


def sources(own, near, far):
    core, half, lo = (lax.axis_index(name) for name in ("core", "half", "lo"))
    kept = core == half
    return (
        (kept, own, lo),
        (kept, near, 1 - lo),
        (jnp.logical_not(kept), near, lo),
        (jnp.logical_not(kept), far, 1 - lo),
    )


def edge_kernel(own_ref, near_ref, far_ref, out):
    core = lax.axis_index("core")
    chans = out.shape[0]
    rows = own_ref.shape[0] // chans
    for wanted, ref, block in sources(own_ref, near_ref, far_ref):
        for c, row in ((0, rows - 1), (1, 0)):

            @pl.when(wanted & (core == c) & (block == 1 - c))
            def _():
                out[...] = ref[pl.ds(row, chans, stride=rows), :]


def rows_kernel(flip, own_ref, near_ref, far_ref, fh, fl, v_ref, out, raw):
    total, chans, cols = raw.shape
    rows = own_ref.shape[0] // chans
    for wanted, ref, block in sources(own_ref, near_ref, far_ref):

        @pl.when(wanted)
        def _():
            for row in range(rows):
                raw[block * rows + row] = ref[pl.ds(row, chans, stride=rows), :]

    for row in range(-1, total + 1):
        inside = 0 <= row < total
        high, low = halves(raw[row] if inside else jnp.zeros((chans, cols), F32))
        for a in range(3):
            to = row + a - 1 if flip else row - a + 1
            if 0 <= to < total:
                wide = slice(to * cols, (to + 1) * cols)
                v_ref[a * chans : (a + 1) * chans, wide] = high
                v_ref[(3 + a) * chans : (4 + a) * chans, wide] = low
    out[...] = product(fh[...], v_ref[...]) + product(fl[...], v_ref[: 3 * chans, :])


def rim(edge, total, flip):
    core = lax.axis_index("core")
    row = (total - 1) * (1 - core)
    tap = 2 * core if flip else 2 * (1 - core)
    return row, tap, halves(edge[...])


def span(at, size):
    return pl.ds(pl.multiple_of(at * size, 128), size)


def layer_grad(out, scale, dh, dl, v_ref, edge, total, flip):
    mine = dh.shape[0] // 3
    chans, cols = edge.shape
    low = v_ref.shape[0] // 2
    nt = ((1,), (1,))
    row, tap, (eh, el) = rim(edge, total, flip)
    wide = span(row, cols)
    grad = dot3(dh[...], dl[...], v_ref[:low, :], v_ref[low:, :], nt)
    extra = dot3(dh[:, wide], dl[:, wide], eh, el, nt)
    for a in range(3):
        part = grad[:, a * chans : (a + 1) * chans]
        if a != 1:
            part = part + jnp.where(tap == a, extra, 0.0)
        for b in range(3):
            t = 3 * a + b
            out[t * mine : (t + 1) * mine, :] = scale * part[b * mine : (b + 1) * mine, :]


def row_sums(scale, wh, wl, ref, edge, total, flip):
    mine = wh.shape[0] // 3
    chans, cols = edge.shape
    row, tap, (eh, el) = rim(edge, total, flip)
    deep = span(tap, chans)
    extra = dot3(wh[:, deep], wl[:, deep], eh, el, ((1,), (0,)))
    side = 1 if flip else -1
    found = []
    for at in range(total):
        wide = slice(at * cols, (at + 1) * cols)
        parts = []
        for b in range(3):
            value = ref[b * mine : (b + 1) * mine, wide]
            if at in (0, total - 1):
                value = value + jnp.where(row == at, extra[b * mine : (b + 1) * mine, :], 0.0)
            parts.append(value)
        found.append(scale * (parts[1] + moved(parts[0], side) + moved(parts[2], -side)))
    return found


def hidden_kernel(total, scale, edge, fh, fl, pre_ref, hh, hl, slope_ref):
    cols = edge.shape[1]
    for row, pre in enumerate(row_sums(scale, fh, fl, pre_ref, edge, total, False)):
        sig = jax.nn.sigmoid(pre)
        hidden = pre * sig
        slope_ref[:, row * cols : (row + 1) * cols] = sig * (1.0 + pre * (1.0 - sig))
        for b, value in enumerate((moved(hidden, -1), hidden, moved(hidden, 1))):
            put(hh, hl, b, row, value)


def either(wanted, scale, out, x_edge, c_edge, xv, cv, hh, hl, dh, dl, total):

    @pl.when(wanted == 0)
    def _():
        layer_grad(out, scale, dh, dl, xv, x_edge, total, False)

    @pl.when(wanted == 1)
    def _():
        layer_grad(out, scale, hh, hl, cv, c_edge, total, True)


def give_kernel(total, scale, *refs):
    x_edge, c_edge, xv, cv, hh, hl, slope_ref, gh, gl, back_ref, give_ref, dh, dl = refs
    cols = x_edge.shape[1]
    for row, dhidden in enumerate(row_sums(scale, gh, gl, back_ref, c_edge, total, True)):
        dpre = dhidden * slope_ref[:, row * cols : (row + 1) * cols]
        for b, value in enumerate((moved(dpre, 1), dpre, moved(dpre, -1))):
            put(dh, dl, b, row, value)
    wanted = 1 - lax.axis_index("core")
    either(wanted, scale, give_ref, x_edge, c_edge, xv, cv, hh, hl, dh, dl, total)


def keep_kernel(total, scale, x_edge, c_edge, xv, cv, hh, hl, dh, dl, keep_ref):
    wanted = lax.axis_index("core")
    either(wanted, scale, keep_ref, x_edge, c_edge, xv, cv, hh, hl, dh, dl, total)


def gram_kernel(v_ref, out):
    count = v_ref.shape[0]
    col = lax.broadcasted_iota(jnp.int32, out.shape, 1)
    total = jnp.zeros(out.shape, F32)
    for i in range(count):
        for j in range(i, count):
            value = jnp.sum(v_ref[i] * v_ref[j], keepdims=True)
            total = jnp.where((col == i * count + j) | (col == j * count + i), value, total)
    out[...] = total


def merge_kernel(n_band, sums_ref, v_ref, out):
    core = lax.axis_index("core")
    count = v_ref.shape[0]
    sums = sums_ref[...]
    lanes = sums.shape[1]
    device = lax.broadcasted_iota(jnp.int32, sums.shape, 0)
    same = ((device // n_band) % 2) == core
    flat = jnp.sum(jnp.where(same, sums, 0.0), 0, keepdims=True)
    row = lax.broadcasted_iota(jnp.int32, (count, lanes), 0)
    col = lax.broadcasted_iota(jnp.int32, (count, lanes), 1)
    gram = jnp.broadcast_to(flat, (count, lanes))
    wide = gram
    for i in range(1, count):
        gram = jnp.where(row == i, pltpu.roll(wide, lanes - i * count, 1), gram)
    gram = jnp.where(col < count, gram, 0.0)

    def swap(value, axis, step):
        size = value.shape[axis]
        index = row if axis == 0 else col
        return jnp.where(
            (index & step) != 0,
            pltpu.roll(value, step, axis),
            pltpu.roll(value, size - step, axis),
        )

    weight = jnp.ones((count, 1), F32)
    step = 1
    while step < count:
        own = jnp.where(row == col, gram, 0.0)
        cross = jnp.where((row ^ step) == col, gram, 0.0)
        down = 1.0 - jnp.sum(cross, 1, keepdims=True) / (
            2.0 * (jnp.sum(own, 1, keepdims=True) + 1e-06)
        )
        along = 1.0 - jnp.sum(cross, 0, keepdims=True) / (
            2.0 * (jnp.sum(own, 0, keepdims=True) + 1e-06)
        )
        weight = weight * down
        gram = gram * down * along
        gram = gram + swap(gram, 0, step)
        gram = gram + swap(gram, 1, step)
        step *= 2
    total = jnp.zeros(out.shape, F32)
    for i in range(count):
        total = total + weight[i : i + 1, :] * v_ref[i]
    out[...] = total


def gather_kernel(*refs):
    parts, out = refs[:-1], refs[-1]
    pair = lax.axis_index("pair")
    size = parts[0].shape[0]
    for k, part in enumerate(parts):
        start = pl.multiple_of(lax.bitwise_xor(pair, k) * size, 8)
        out[pl.ds(start, size), :] = part[...]


def new_layer(n_pair, n_lo, layer, rates_ref, f_ref, pieces, held, fresh):
    band = lax.axis_index("half") * n_lo + lax.axis_index("lo")
    size = pieces[0].shape[0] // n_pair
    chans = f_ref.shape[2]
    mine = chans // n_lo
    for k, piece in enumerate(pieces):
        place = lax.bitwise_xor(band, k)
        half, lo = place // n_lo, place % n_lo
        for p in range(n_pair):
            to = pl.ds(pl.multiple_of((2 * p + half) * size, 8), size)
            held[lo, to, :] = piece[p * size : (p + 1) * size, :]
    for l in range(2):

        @pl.when(layer == l)
        def _():
            rate = rates_ref[l]
            for t in range(9):
                at = pl.ds(t, chans, stride=9)
                value = held[:, t * mine : (t + 1) * mine, :].reshape(chans, chans)
                if l == 0:
                    value = value.T
                fresh[at, :] = f_ref[l, at, :] - rate * value


def own_kernel(n_pair, n_lo, rates_ref, f_ref, *refs):
    pieces, (fresh, held) = refs[:-2], refs[-2:]
    new_layer(n_pair, n_lo, lax.axis_index("core"), rates_ref, f_ref, pieces, held, fresh)


def final_kernel(n_pair, n_lo, rates_ref, f_ref, mine_ref, *refs):
    pieces, (out, held, fresh, sems) = refs[:-4], refs[-4:]
    core = lax.axis_index("core")
    first = pltpu.make_async_copy(mine_ref, out.at[0, core], sems.at[0])
    first.start()
    new_layer(n_pair, n_lo, 1 - core, rates_ref, f_ref, pieces, held, fresh)
    second = pltpu.make_async_copy(fresh, out.at[0, 1 - core], sems.at[1])
    second.start()
    first.wait()
    second.wait()


def xor_route(count, k):
    return [(i, i ^ k) for i in range(count)]


def swapped(value, axis, k):
    return lax.ppermute(value, axis, xor_route(lax.axis_size(axis), k))


def routes():
    def at(core, half, lo):
        return (core * 2 + half) * 2 + lo

    every = [(core, half, lo) for core in range(2) for half in range(2) for lo in range(2)]
    near = [(at(c, h, l), at(h, c, 1 - l if c == h else l)) for c, h, l in every]
    far = [(at(c, h, l), at(h, c, 1 - l)) for c, h, l in every if c != h]
    onward = [(at(c, h, l), at(c, h, 1 - l)) for c, h, l in every if c != h]
    return near, far, onward


def sent(value, route):
    return lax.ppermute(value, ("core", "half", "lo"), route)


def fast(images, cotangent, filters, rates):
    _, chans, rows, cols = images.shape
    n_pair, n_lo = lax.axis_size("pair"), lax.axis_size("lo")
    n_image, n_band = 2 * n_pair, 2 * n_lo
    kdim = filters.shape[1]
    mine = chans // n_lo
    total = n_lo * rows
    slot = 9 * mine // n_image
    flat = (chans * rows, cols)
    bf = lambda *shape: jax.ShapeDtypeStruct(shape, BF16)
    tall, thin, wide = 3 * chans, 3 * mine, total * cols
    near, far, onward = routes()
    c_near = sent(cotangent, near)
    x_near = sent(images, near)
    x_far = sent(images, far)
    c_far = sent(c_near, onward)
    xs = [v.reshape(flat) for v in (images, x_near, x_far)]
    cs = [v.reshape(flat) for v in (cotangent, c_near, c_far)]
    fh, fl, gh, gl = call(
        filter_kernel,
        [bf(thin, 2 * tall), bf(thin, tall)] * 2,
        [pltpu.VMEM((2, 9, chans, chans), F32)],
    )(filters)
    (edge,) = call(edge_kernel, [(chans, cols)])(*xs)
    x_edge = swapped(edge, "core", 1)
    raw = [pltpu.VMEM((total, chans, cols), F32)]
    work = 6 * thin * tall * wide
    outs = [bf(2 * tall, wide), (thin, wide)]
    xv, pre = call(functools.partial(rows_kernel, False), outs, raw, flops=work)(*xs, fh, fl)
    scale = kdim ** (-0.5)
    hh, hl, slope = call(
        functools.partial(hidden_kernel, total, scale), [bf(thin, wide)] * 2 + [(mine, wide)]
    )(x_edge, fh, fl, pre)
    (edge,) = call(edge_kernel, [(chans, cols)])(*cs)
    c_edge = swapped(edge, "core", 1)
    cv, back = call(functools.partial(rows_kernel, True), outs, raw, flops=work)(*cs, gh, gl)
    rows_of = (x_edge, c_edge, xv, cv, hh, hl)
    part = (9 * mine, chans)
    give, dh, dl = call(
        functools.partial(give_kernel, total, scale), [part] + [bf(thin, wide)] * 2, flops=2 * work
    )(*rows_of, slope, gh, gl, back)
    given = swapped(give, "core", 1)
    (keep,) = call(
        functools.partial(keep_kernel, total, scale), [part], flops=work
    )(*rows_of, dh, dl)
    whole = keep + given
    slices = lax.all_to_all(
        whole.reshape(n_image, slot, chans), ("pair", "half"), 0, 0, tiled=True
    )
    (gram,) = call(gram_kernel, [(1, 128)])(slices)
    sums = jnp.broadcast_to(gram, (n_image * n_band, gram.shape[1]))
    sums = lax.all_to_all(sums, AXES, 0, 0, tiled=True)
    (merged,) = call(functools.partial(merge_kernel, n_band), [(slot, chans)])(sums, slices)
    pieces = [merged] + [swapped(merged, "pair", k) for k in range(1, n_pair)]
    (block,) = call(gather_kernel, [(n_pair * slot, chans)])(*pieces)
    own = [block] + [swapped(block, ("half", "lo"), k) for k in range(1, n_band)]
    others = [swapped(piece, "core", 1) for piece in own]
    layer = (kdim, chans)
    held = pltpu.VMEM((n_lo,) + part, F32)
    vmem, smem = (pl.BlockSpec(memory_space=m) for m in (pltpu.VMEM, pltpu.SMEM))
    params = pltpu.CompilerParams(vmem_limit_bytes=40 * 2**20)
    fresh = pl.pallas_call(
        functools.partial(own_kernel, n_pair, n_lo),
        out_shape=jax.ShapeDtypeStruct(layer, F32),
        in_specs=[smem] + [vmem] * (1 + n_band),
        out_specs=vmem,
        scratch_shapes=[held],
        compiler_params=params,
    )(rates, filters, *own)
    return pl.pallas_call(
        functools.partial(final_kernel, n_pair, n_lo),
        out_shape=jax.ShapeDtypeStruct((1,) + filters.shape, F32),
        in_specs=[smem] + [vmem] * (2 + n_band),
        out_specs=pl.BlockSpec(memory_space=pl.ANY),
        scratch_shapes=[held, pltpu.VMEM(layer, F32), pltpu.SemaphoreType.DMA((2,))],
        compiler_params=params,
    )(rates, filters, fresh, *others)


def with_rims(field):
    count = lax.axis_size("band")
    forward = [(i, i + 1) for i in range(count - 1)]
    backward = [(target, source) for source, target in forward]
    low = lax.ppermute(field[:, -1:], "band", forward)
    high = lax.ppermute(field[:, :1], "band", backward)
    extended = jnp.concatenate([low, field, high], axis=1)
    return jnp.pad(extended, ((0, 0), (0, 0), (1, 1)))


def taps(padded, rows, cols, flip=False):
    chans = padded.shape[0]
    at = (2, 1, 0) if flip else (0, 1, 2)
    pieces = [padded[:, dr : dr + rows, dc : dc + cols] for dr in at for dc in at]
    return jnp.stack(pieces, axis=1).reshape(chans, 9, rows * cols)


def plain(images, cotangent, filters, rates):
    feats, cot = images[0], cotangent[0]
    chans, rows, cols = feats.shape
    scale = (9 * chans) ** (-0.5)
    patch_one = taps(with_rims(feats), rows, cols).reshape(9 * chans, rows * cols)
    pre = scale * jnp.einsum("kc,kp->cp", filters[0], patch_one, precision=HIGH)
    hidden = jax.nn.silu(pre).reshape(chans, rows, cols)
    patch_two = taps(with_rims(hidden), rows, cols).reshape(9 * chans, rows * cols)
    back = taps(with_rims(cot), rows, cols, flip=True)
    flat_cot = cot.reshape(chans, rows * cols)
    grad_two = scale * jnp.einsum("kp,cp->kc", patch_two, flat_cot, precision=HIGH)
    weight_two = filters[1].reshape(chans, 9, chans)
    dhidden = scale * jnp.einsum("itc,ctp->ip", weight_two, back, precision=HIGH)
    sig = jax.nn.sigmoid(pre)
    dpre = dhidden * sig * (1.0 + pre * (1.0 - sig))
    grad_one = scale * jnp.einsum("kp,cp->kc", patch_one, dpre, precision=HIGH)
    block = lax.psum_scatter(
        jnp.stack([grad_one, grad_two]), "band", scatter_dimension=1, tiled=True
    )
    count = lax.axis_size("image")
    for level in range(count.bit_length() - 1):
        other = lax.ppermute(block, "image", xor_route(count, 1 << level))
        inner, own_sq, other_sq = lax.psum(
            tuple(jnp.sum(v, axis=(1, 2)) for v in (block * other, block * block, other * other)),
            "band",
        )
        low = (1.0 - inner / (2.0 * (own_sq + 1e-06)))[:, None, None]
        high = (1.0 - inner / (2.0 * (other_sq + 1e-06)))[:, None, None]
        block = low * block + high * other
    height = block.shape[1]
    mine = lax.dynamic_slice_in_dim(filters, lax.axis_index("band") * height, height, 1)
    fresh = (mine - rates[:, None, None] * block)[None]
    return lax.all_gather(fresh, "band", axis=2, tiled=True)


def power_of_two(n):
    return n & (n - 1) == 0


def solution(mesh):
    n_image, n_band = mesh.shape["image"], mesh.shape["band"]

    def step(images, cotangent, filters, rates):
        chans = images.shape[1]
        if (
            4 <= n_image
            and n_image**2 <= 128
            and n_band == 4
            and power_of_two(n_image)
            and (9 * chans) % (n_band // 2 * n_image * 8) == 0
        ):
            shape = (n_image // 2, 2, 2, n_band // 2)
            split = jax.sharding.Mesh(mesh.devices.reshape(shape), AXES)
            image, band = ("pair", "core"), ("half", "lo")

            def body(*args):
                return fast(*args)

        else:
            split, image, band, body = mesh, "image", "band", plain
        whole = jax.shard_map(
            body,
            mesh=split,
            in_specs=(P(image, None, band, None), P(image, None, band, None), P(), P()),
            out_specs=P(image, None, None, None),
            check_vma=False,
        )
        return whole(images, cotangent, filters, rates)

    return step
```

```python
import functools

import jax
import jax.numpy as jnp
from jax import lax
from jax.experimental import pallas as pl
from jax.experimental.pallas import tpu as pltpu
from jax.sharding import PartitionSpec as P


HIGH = lax.Precision.HIGHEST
F32 = jnp.float32
BF16 = jnp.bfloat16


AXES = ("pair", "core", "half", "lo")


def call(body, outs, scratch=(), flops=0):
    outs = [o if isinstance(o, jax.ShapeDtypeStruct) else jax.ShapeDtypeStruct(o, F32) for o in outs]
    return pl.pallas_call(
        body,
        out_shape=outs,
        scratch_shapes=list(scratch),
        cost_estimate=pl.CostEstimate(flops=flops, bytes_accessed=flops // 500, transcendentals=0),
        compiler_params=pltpu.CompilerParams(vmem_limit_bytes=40 * 2**20),
    )


def halves(value):
    high = value.astype(BF16)
    return high, (value - high.astype(F32)).astype(BF16)


def dot3(ah, al, bh, bl, dims):
    def one(a, b):
        return lax.dot_general(a, b, (dims, ((), ())), preferred_element_type=F32)

    return one(ah, bh) + (one(ah, bl) + one(al, bh))


def moved(value, step):
    cols = value.shape[-1]
    col = lax.broadcasted_iota(jnp.int32, value.shape, value.ndim - 1)
    if step > 0:
        return jnp.where(col == cols - 1, 0.0, pltpu.roll(value, cols - 1, 1))
    return jnp.where(col == 0, 0.0, pltpu.roll(value, 1, 1))


def put(high_ref, low_ref, at, row, value):
    high, low = halves(value)
    rows, cols = value.shape
    part = (slice(at * rows, (at + 1) * rows), slice(row * cols, (row + 1) * cols))
    high_ref[part] = high
    low_ref[part] = low


def filter_kernel(f_ref, fh, fl, gh, gl, part_ref, taps_ref):
    lo = lax.axis_index("lo")
    chans = f_ref.shape[2]
    mine = fh.shape[0] // 3
    rows = pl.ds(pl.multiple_of(lo * mine, 8), mine)
    for a in range(3):
        for b in range(3):
            t = 3 * a + b
            at = pl.ds(t, chans, stride=9)
            taps_ref[0, t] = f_ref[0, at, :].T
            taps_ref[1, t] = f_ref[1, at, :]
            put(fh, fl, b, a, taps_ref[0, t, rows, :])
            put(gh, gl, b, a, taps_ref[1, t, rows, :])
            for layer in range(2):
                part_ref[layer, t * mine : (t + 1) * mine, :] = taps_ref[layer, t, rows, :]


def sources(own, near, far):
    core, half, lo = (lax.axis_index(name) for name in ("core", "half", "lo"))
    kept = core == half
    return (
        (kept, own, lo),
        (kept, near, 1 - lo),
        (jnp.logical_not(kept), near, lo),
        (jnp.logical_not(kept), far, 1 - lo),
    )


def edge_kernel(own_ref, near_ref, far_ref, out):
    core = lax.axis_index("core")
    chans = out.shape[0]
    rows = own_ref.shape[0] // chans
    for wanted, ref, block in sources(own_ref, near_ref, far_ref):
        for c, row in ((0, rows - 1), (1, 0)):

            @pl.when(wanted & (core == c) & (block == 1 - c))
            def _():
                out[...] = ref[pl.ds(row, chans, stride=rows), :]


def rows_kernel(flip, own_ref, near_ref, far_ref, fh, fl, vh, vl, out, raw):
    total, chans, cols = raw.shape
    rows = own_ref.shape[0] // chans
    for wanted, ref, block in sources(own_ref, near_ref, far_ref):

        @pl.when(wanted)
        def _():
            for row in range(rows):
                raw[block * rows + row] = ref[pl.ds(row, chans, stride=rows), :]

    for a in range(3):
        step = 1 - a if flip else a - 1
        for row in range(total):
            value = raw[row + step] if 0 <= row + step < total else jnp.zeros((chans, cols), F32)
            put(vh, vl, a, row, value)
    out[...] = dot3(fh[...], fl[...], vh[...], vl[...], ((1,), (0,)))


def rims(edge, first, final, last):
    core = lax.axis_index("core")
    before = halves(jnp.where(core == 1, edge[...], 0.0))
    after = halves(jnp.where(core == 0, edge[...], 0.0))
    return {first: (0, before), final: (last, after)}


def layer_grad(out, scale, dh, dl, vh, vl, rim_of):
    mine = dh.shape[0] // 3
    chans, cols = rim_of[0][1][0].shape
    grad = dot3(dh[...], dl[...], vh[...], vl[...], ((1,), (1,)))
    for a in range(3):
        part = grad[:, a * chans : (a + 1) * chans]
        if a in rim_of:
            row, rim = rim_of[a]
            wide = slice(row * cols, (row + 1) * cols)
            part = part + dot3(dh[:, wide], dl[:, wide], *rim, ((1,), (1,)))
        for b in range(3):
            t = 3 * a + b
            out[t * mine : (t + 1) * mine, :] = scale * part[b * mine : (b + 1) * mine, :]


def row_sums(scale, wh, wl, ref, rim_of, total, flip):
    mine = wh.shape[0] // 3
    chans, cols = rim_of[0][1][0].shape
    rim_row = {
        row: dot3(
            wh[:, a * chans : (a + 1) * chans],
            wl[:, a * chans : (a + 1) * chans],
            *rim,
            ((1,), (0,)),
        )
        for a, (row, rim) in rim_of.items()
    }
    side = 1 if flip else -1
    found = []
    for row in range(total):
        wide = slice(row * cols, (row + 1) * cols)
        parts = []
        for b in range(3):
            value = ref[b * mine : (b + 1) * mine, wide]
            if row in rim_row:
                value = value + rim_row[row][b * mine : (b + 1) * mine, :]
            parts.append(value)
        found.append(scale * (parts[1] + moved(parts[0], side) + moved(parts[2], -side)))
    return found


def hidden_kernel(total, scale, edge, fh, fl, pre_ref, hh, hl, slope_ref):
    cols = edge.shape[1]
    for row, pre in enumerate(
        row_sums(scale, fh, fl, pre_ref, rims(edge, 0, 2, total - 1), total, False)
    ):
        sig = jax.nn.sigmoid(pre)
        hidden = pre * sig
        slope_ref[:, row * cols : (row + 1) * cols] = sig * (1.0 + pre * (1.0 - sig))
        for b, value in enumerate((moved(hidden, -1), hidden, moved(hidden, 1))):
            put(hh, hl, b, row, value)


def either(wanted, scale, out, x_edge, c_edge, xh, xl, ch, cl, hh, hl, dh, dl, last):

    @pl.when(wanted == 0)
    def _():
        layer_grad(out, scale, dh, dl, xh, xl, rims(x_edge, 0, 2, last))

    @pl.when(wanted == 1)
    def _():
        layer_grad(out, scale, hh, hl, ch, cl, rims(c_edge, 2, 0, last))


def give_kernel(total, scale, *refs):
    x_edge, c_edge, xh, xl, ch, cl, hh, hl, slope_ref, gh, gl, back_ref = refs[:12]
    give_ref, dh, dl = refs[12:]
    cols = x_edge.shape[1]
    for row, dhidden in enumerate(
        row_sums(scale, gh, gl, back_ref, rims(c_edge, 2, 0, total - 1), total, True)
    ):
        dpre = dhidden * slope_ref[:, row * cols : (row + 1) * cols]
        for b, value in enumerate((moved(dpre, 1), dpre, moved(dpre, -1))):
            put(dh, dl, b, row, value)
    wanted = 1 - lax.axis_index("core")
    either(wanted, scale, give_ref, x_edge, c_edge, xh, xl, ch, cl, hh, hl, dh, dl, total - 1)


def keep_kernel(total, scale, *refs):
    x_edge, c_edge, xh, xl, ch, cl, hh, hl, dh, dl, keep_ref = refs
    wanted = lax.axis_index("core")
    either(wanted, scale, keep_ref, x_edge, c_edge, xh, xl, ch, cl, hh, hl, dh, dl, total - 1)


def gram_kernel(v_ref, out):
    count = v_ref.shape[0]
    col = lax.broadcasted_iota(jnp.int32, out.shape, 1)
    total = jnp.zeros(out.shape, F32)
    for i in range(count):
        for j in range(i, count):
            value = jnp.sum(v_ref[i] * v_ref[j], keepdims=True)
            total = jnp.where((col == i * count + j) | (col == j * count + i), value, total)
    out[...] = total


def merge_kernel(n_band, rates_ref, sums_ref, v_ref, f_ref, out):
    core = lax.axis_index("core")
    count = v_ref.shape[0]
    sums = sums_ref[...]
    lanes = sums.shape[1]
    device = lax.broadcasted_iota(jnp.int32, sums.shape, 0)
    same = ((device // n_band) % 2) == core
    flat = jnp.sum(jnp.where(same, sums, 0.0), 0, keepdims=True)
    row = lax.broadcasted_iota(jnp.int32, (count, lanes), 0)
    col = lax.broadcasted_iota(jnp.int32, (count, lanes), 1)
    gram = jnp.broadcast_to(flat, (count, lanes))
    wide = gram
    for i in range(1, count):
        gram = jnp.where(row == i, pltpu.roll(wide, lanes - i * count, 1), gram)
    gram = jnp.where(col < count, gram, 0.0)

    def swap(value, axis, step):
        size = value.shape[axis]
        index = row if axis == 0 else col
        return jnp.where(
            (index & step) != 0,
            pltpu.roll(value, step, axis),
            pltpu.roll(value, size - step, axis),
        )

    weight = jnp.ones((count, 1), F32)
    step = 1
    while step < count:
        own = jnp.where(row == col, gram, 0.0)
        cross = jnp.where((row ^ step) == col, gram, 0.0)
        down = 1.0 - jnp.sum(cross, 1, keepdims=True) / (
            2.0 * (jnp.sum(own, 1, keepdims=True) + 1e-06)
        )
        along = 1.0 - jnp.sum(cross, 0, keepdims=True) / (
            2.0 * (jnp.sum(own, 0, keepdims=True) + 1e-06)
        )
        weight = weight * down
        gram = gram * down * along
        gram = gram + swap(gram, 0, step)
        gram = gram + swap(gram, 1, step)
        step *= 2
    total = jnp.zeros(out.shape, F32)
    for i in range(count):
        total = total + weight[i : i + 1, :] * v_ref[i]
    size = out.shape[0]
    slot = 2 * lax.axis_index("pair") + lax.axis_index("half")
    mine = f_ref[core, pl.ds(pl.multiple_of(slot * size, 8), size), :]
    out[...] = mine - rates_ref[core] * total


def gather_kernel(*refs):
    parts, out = refs[:-1], refs[-1]
    pair = lax.axis_index("pair")
    size = parts[0].shape[0]
    for k, part in enumerate(parts):
        start = pl.multiple_of(lax.bitwise_xor(pair, k) * size, 8)
        out[pl.ds(start, size), :] = part[...]


def new_layer(n_pair, n_lo, layer, pieces, held, fresh):
    band = lax.axis_index("half") * n_lo + lax.axis_index("lo")
    size = pieces[0].shape[0] // n_pair
    chans = fresh.shape[1]
    mine = chans // n_lo
    for k, piece in enumerate(pieces):
        place = lax.bitwise_xor(band, k)
        half, lo = place // n_lo, place % n_lo
        for p in range(n_pair):
            to = pl.ds(pl.multiple_of((2 * p + half) * size, 8), size)
            held[lo, to, :] = piece[p * size : (p + 1) * size, :]
    for l in range(2):

        @pl.when(layer == l)
        def _():
            for t in range(9):
                at = pl.ds(t, chans, stride=9)
                value = held[:, t * mine : (t + 1) * mine, :].reshape(chans, chans)
                if l == 0:
                    value = value.T
                fresh[at, :] = value


def own_kernel(n_pair, n_lo, *refs):
    pieces, (fresh, held) = refs[:-2], refs[-2:]
    new_layer(n_pair, n_lo, lax.axis_index("core"), pieces, held, fresh)


def final_kernel(n_pair, n_lo, mine_ref, *refs):
    pieces, (out, held, fresh, sems) = refs[:-4], refs[-4:]
    core = lax.axis_index("core")
    first = pltpu.make_async_copy(mine_ref, out.at[0, core], sems.at[0])
    first.start()
    new_layer(n_pair, n_lo, 1 - core, pieces, held, fresh)
    second = pltpu.make_async_copy(fresh, out.at[0, 1 - core], sems.at[1])
    second.start()
    first.wait()
    second.wait()


def xor_route(count, k):
    return [(i, i ^ k) for i in range(count)]


def swapped(value, axis, k):
    return lax.ppermute(value, axis, xor_route(lax.axis_size(axis), k))


def routes():
    def at(core, half, lo):
        return (core * 2 + half) * 2 + lo

    every = [(core, half, lo) for core in range(2) for half in range(2) for lo in range(2)]
    near = [(at(c, h, l), at(h, c, 1 - l if c == h else l)) for c, h, l in every]
    far = [(at(c, h, l), at(h, c, 1 - l)) for c, h, l in every if c != h]
    onward = [(at(c, h, l), at(c, h, 1 - l)) for c, h, l in every if c != h]
    return near, far, onward


def sent(value, route):
    return lax.ppermute(value, ("core", "half", "lo"), route)


def fast(images, cotangent, filters, rates):
    _, chans, rows, cols = images.shape
    n_pair, n_lo = lax.axis_size("pair"), lax.axis_size("lo")
    n_image, n_band = 2 * n_pair, 2 * n_lo
    kdim = filters.shape[1]
    mine = chans // n_lo
    total = n_lo * rows
    slot = 9 * mine // n_image
    flat = (chans * rows, cols)
    bf = lambda *shape: jax.ShapeDtypeStruct(shape, BF16)
    tall, thin, wide = 3 * chans, 3 * mine, total * cols
    near, far, onward = routes()
    c_near = sent(cotangent, near)
    x_near = sent(images, near)
    x_far = sent(images, far)
    c_far = sent(c_near, onward)
    xs = [v.reshape(flat) for v in (images, x_near, x_far)]
    cs = [v.reshape(flat) for v in (cotangent, c_near, c_far)]
    fh, fl, gh, gl, tapped = call(
        filter_kernel,
        [bf(thin, tall)] * 4 + [(2, 9 * mine, chans)],
        [pltpu.VMEM((2, 9, chans, chans), F32)],
    )(filters)
    (edge,) = call(edge_kernel, [(chans, cols)])(*xs)
    x_edge = swapped(edge, "core", 1)
    raw = [pltpu.VMEM((total, chans, cols), F32)]
    work = 6 * thin * tall * wide
    outs = [bf(tall, wide)] * 2 + [(thin, wide)]
    xh, xl, pre = call(functools.partial(rows_kernel, False), outs, raw, flops=work)(*xs, fh, fl)
    scale = kdim ** (-0.5)
    hh, hl, slope = call(
        functools.partial(hidden_kernel, total, scale), [bf(thin, wide)] * 2 + [(mine, wide)]
    )(x_edge, fh, fl, pre)
    (edge,) = call(edge_kernel, [(chans, cols)])(*cs)
    c_edge = swapped(edge, "core", 1)
    ch, cl, back = call(functools.partial(rows_kernel, True), outs, raw, flops=work)(*cs, gh, gl)
    rows_of = (x_edge, c_edge, xh, xl, ch, cl, hh, hl)
    part = (9 * mine, chans)
    give, dh, dl = call(
        functools.partial(give_kernel, total, scale), [part] + [bf(thin, wide)] * 2, flops=2 * work
    )(*rows_of, slope, gh, gl, back)
    given = swapped(give, "core", 1)
    (keep,) = call(
        functools.partial(keep_kernel, total, scale), [part], flops=work
    )(*rows_of, dh, dl)
    whole = keep + given
    slices = lax.all_to_all(
        whole.reshape(n_image, slot, chans), ("pair", "half"), 0, 0, tiled=True
    )
    (gram,) = call(gram_kernel, [(1, 128)])(slices)
    sums = jnp.broadcast_to(gram, (n_image * n_band, gram.shape[1]))
    sums = lax.all_to_all(sums, AXES, 0, 0, tiled=True)
    vmem, smem = (pl.BlockSpec(memory_space=m) for m in (pltpu.VMEM, pltpu.SMEM))
    params = pltpu.CompilerParams(vmem_limit_bytes=40 * 2**20)
    merged = pl.pallas_call(
        functools.partial(merge_kernel, n_band),
        out_shape=jax.ShapeDtypeStruct((slot, chans), F32),
        in_specs=[smem] + [vmem] * 3,
        out_specs=vmem,
        compiler_params=params,
    )(rates, sums, slices, tapped)
    pieces = [merged] + [swapped(merged, "pair", k) for k in range(1, n_pair)]
    (block,) = call(gather_kernel, [(n_pair * slot, chans)])(*pieces)
    own = [block] + [swapped(block, ("half", "lo"), k) for k in range(1, n_band)]
    others = [swapped(piece, "core", 1) for piece in own]
    layer = (kdim, chans)
    held = pltpu.VMEM((n_lo,) + part, F32)
    fresh = pl.pallas_call(
        functools.partial(own_kernel, n_pair, n_lo),
        out_shape=jax.ShapeDtypeStruct(layer, F32),
        in_specs=[vmem] * n_band,
        out_specs=vmem,
        scratch_shapes=[held],
        compiler_params=params,
    )(*own)
    return pl.pallas_call(
        functools.partial(final_kernel, n_pair, n_lo),
        out_shape=jax.ShapeDtypeStruct((1,) + filters.shape, F32),
        in_specs=[vmem] * (1 + n_band),
        out_specs=pl.BlockSpec(memory_space=pl.ANY),
        scratch_shapes=[held, pltpu.VMEM(layer, F32), pltpu.SemaphoreType.DMA((2,))],
        compiler_params=params,
    )(fresh, *others)


def with_rims(field):
    count = lax.axis_size("band")
    forward = [(i, i + 1) for i in range(count - 1)]
    backward = [(target, source) for source, target in forward]
    low = lax.ppermute(field[:, -1:], "band", forward)
    high = lax.ppermute(field[:, :1], "band", backward)
    extended = jnp.concatenate([low, field, high], axis=1)
    return jnp.pad(extended, ((0, 0), (0, 0), (1, 1)))


def taps(padded, rows, cols, flip=False):
    chans = padded.shape[0]
    at = (2, 1, 0) if flip else (0, 1, 2)
    pieces = [padded[:, dr : dr + rows, dc : dc + cols] for dr in at for dc in at]
    return jnp.stack(pieces, axis=1).reshape(chans, 9, rows * cols)


def plain(images, cotangent, filters, rates):
    feats, cot = images[0], cotangent[0]
    chans, rows, cols = feats.shape
    scale = (9 * chans) ** (-0.5)
    patch_one = taps(with_rims(feats), rows, cols).reshape(9 * chans, rows * cols)
    pre = scale * jnp.einsum("kc,kp->cp", filters[0], patch_one, precision=HIGH)
    hidden = jax.nn.silu(pre).reshape(chans, rows, cols)
    patch_two = taps(with_rims(hidden), rows, cols).reshape(9 * chans, rows * cols)
    back = taps(with_rims(cot), rows, cols, flip=True)
    flat_cot = cot.reshape(chans, rows * cols)
    grad_two = scale * jnp.einsum("kp,cp->kc", patch_two, flat_cot, precision=HIGH)
    weight_two = filters[1].reshape(chans, 9, chans)
    dhidden = scale * jnp.einsum("itc,ctp->ip", weight_two, back, precision=HIGH)
    sig = jax.nn.sigmoid(pre)
    dpre = dhidden * sig * (1.0 + pre * (1.0 - sig))
    grad_one = scale * jnp.einsum("kp,cp->kc", patch_one, dpre, precision=HIGH)
    block = lax.psum_scatter(
        jnp.stack([grad_one, grad_two]), "band", scatter_dimension=1, tiled=True
    )
    count = lax.axis_size("image")
    for level in range(count.bit_length() - 1):
        other = lax.ppermute(block, "image", xor_route(count, 1 << level))
        inner, own_sq, other_sq = lax.psum(
            tuple(jnp.sum(v, axis=(1, 2)) for v in (block * other, block * block, other * other)),
            "band",
        )
        low = (1.0 - inner / (2.0 * (own_sq + 1e-06)))[:, None, None]
        high = (1.0 - inner / (2.0 * (other_sq + 1e-06)))[:, None, None]
        block = low * block + high * other
    height = block.shape[1]
    mine = lax.dynamic_slice_in_dim(filters, lax.axis_index("band") * height, height, 1)
    fresh = (mine - rates[:, None, None] * block)[None]
    return lax.all_gather(fresh, "band", axis=2, tiled=True)


def power_of_two(n):
    return n & (n - 1) == 0


def solution(mesh):
    n_image, n_band = mesh.shape["image"], mesh.shape["band"]

    def step(images, cotangent, filters, rates):
        chans = images.shape[1]
        if (
            4 <= n_image
            and n_image**2 <= 128
            and n_band == 4
            and power_of_two(n_image)
            and (9 * chans) % (n_band // 2 * n_image * 8) == 0
        ):
            shape = (n_image // 2, 2, 2, n_band // 2)
            split = jax.sharding.Mesh(mesh.devices.reshape(shape), AXES)
            image, band = ("pair", "core"), ("half", "lo")

            def body(*args):
                return fast(*args)

        else:
            split, image, band, body = mesh, "image", "band", plain
        whole = jax.shard_map(
            body,
            mesh=split,
            in_specs=(P(image, None, band, None), P(image, None, band, None), P(), P()),
            out_specs=P(image, None, None, None),
            check_vma=False,
        )
        return whole(images, cotangent, filters, rates)

    return step
```

```python
import functools

import jax
import jax.numpy as jnp
from jax import lax
from jax.experimental import pallas as pl
from jax.experimental.pallas import tpu as pltpu
from jax.sharding import PartitionSpec as P


HIGH = lax.Precision.HIGHEST
F32 = jnp.float32
BF16 = jnp.bfloat16


AXES = ("pair", "core", "half", "lo")


def call(body, outs, scratch=(), flops=0):
    outs = [o if isinstance(o, jax.ShapeDtypeStruct) else jax.ShapeDtypeStruct(o, F32) for o in outs]
    return pl.pallas_call(
        body,
        out_shape=outs,
        scratch_shapes=list(scratch),
        cost_estimate=pl.CostEstimate(flops=flops, bytes_accessed=flops // 500, transcendentals=0),
        compiler_params=pltpu.CompilerParams(vmem_limit_bytes=40 * 2**20),
    )


def halves(value):
    high = value.astype(BF16)
    return high, (value - high.astype(F32)).astype(BF16)


def dot3(ah, al, bh, bl, dims):
    def one(a, b):
        return lax.dot_general(a, b, (dims, ((), ())), preferred_element_type=F32)

    return one(ah, bh) + (one(ah, bl) + one(al, bh))


def moved(value, step):
    cols = value.shape[-1]
    col = lax.broadcasted_iota(jnp.int32, value.shape, value.ndim - 1)
    if step > 0:
        return jnp.where(col == cols - 1, 0.0, pltpu.roll(value, cols - 1, 1))
    return jnp.where(col == 0, 0.0, pltpu.roll(value, 1, 1))


def put(high_ref, low_ref, at, row, value):
    high, low = halves(value)
    rows, cols = value.shape
    part = (slice(at * rows, (at + 1) * rows), slice(row * cols, (row + 1) * cols))
    high_ref[part] = high
    low_ref[part] = low


def filter_kernel(rates_ref, f_ref, fh, fl, gh, gl, slice_ref, rate_ref, taps_ref, part_ref):
    lo = lax.axis_index("lo")
    chans = f_ref.shape[2]
    mine = fh.shape[0] // 3
    rows = pl.ds(pl.multiple_of(lo * mine, 8), mine)
    for a in range(3):
        for b in range(3):
            t = 3 * a + b
            at = pl.ds(t, chans, stride=9)
            taps_ref[0, t] = f_ref[0, at, :].T
            taps_ref[1, t] = f_ref[1, at, :]
            put(fh, fl, b, a, taps_ref[0, t, rows, :])
            put(gh, gl, b, a, taps_ref[1, t, rows, :])
            for layer in range(2):
                part_ref[layer, t * mine : (t + 1) * mine, :] = taps_ref[layer, t, rows, :]
    core = lax.axis_index("core")
    size = slice_ref.shape[0]
    slot = 2 * lax.axis_index("pair") + lax.axis_index("half")
    slice_ref[...] = part_ref[core, pl.ds(pl.multiple_of(slot * size, 8), size), :]
    rate_ref[...] = jnp.full(rate_ref.shape, rates_ref[core], F32)


def sources(own, near, far):
    core, half, lo = (lax.axis_index(name) for name in ("core", "half", "lo"))
    kept = core == half
    return (
        (kept, own, lo),
        (kept, near, 1 - lo),
        (jnp.logical_not(kept), near, lo),
        (jnp.logical_not(kept), far, 1 - lo),
    )


def edge_kernel(own_ref, near_ref, far_ref, out):
    core = lax.axis_index("core")
    chans = out.shape[0]
    rows = own_ref.shape[0] // chans
    for wanted, ref, block in sources(own_ref, near_ref, far_ref):
        for c, row in ((0, rows - 1), (1, 0)):

            @pl.when(wanted & (core == c) & (block == 1 - c))
            def _():
                out[...] = ref[pl.ds(row, chans, stride=rows), :]


def rows_kernel(flip, own_ref, near_ref, far_ref, fh, fl, vh, vl, out, raw):
    total, chans, cols = raw.shape
    rows = own_ref.shape[0] // chans
    for wanted, ref, block in sources(own_ref, near_ref, far_ref):

        @pl.when(wanted)
        def _():
            for row in range(rows):
                raw[block * rows + row] = ref[pl.ds(row, chans, stride=rows), :]

    for a in range(3):
        step = 1 - a if flip else a - 1
        for row in range(total):
            value = raw[row + step] if 0 <= row + step < total else jnp.zeros((chans, cols), F32)
            put(vh, vl, a, row, value)
    out[...] = dot3(fh[...], fl[...], vh[...], vl[...], ((1,), (0,)))


def rims(edge, first, final, last):
    core = lax.axis_index("core")
    before = halves(jnp.where(core == 1, edge[...], 0.0))
    after = halves(jnp.where(core == 0, edge[...], 0.0))
    return {first: (0, before), final: (last, after)}


def layer_grad(out, scale, dh, dl, vh, vl, rim_of):
    mine = dh.shape[0] // 3
    chans, cols = rim_of[0][1][0].shape
    grad = dot3(dh[...], dl[...], vh[...], vl[...], ((1,), (1,)))
    for a in range(3):
        part = grad[:, a * chans : (a + 1) * chans]
        if a in rim_of:
            row, rim = rim_of[a]
            wide = slice(row * cols, (row + 1) * cols)
            part = part + dot3(dh[:, wide], dl[:, wide], *rim, ((1,), (1,)))
        for b in range(3):
            t = 3 * a + b
            out[t * mine : (t + 1) * mine, :] = scale * part[b * mine : (b + 1) * mine, :]


def row_sums(scale, wh, wl, ref, rim_of, total, flip):
    mine = wh.shape[0] // 3
    chans, cols = rim_of[0][1][0].shape
    rim_row = {
        row: dot3(
            wh[:, a * chans : (a + 1) * chans],
            wl[:, a * chans : (a + 1) * chans],
            *rim,
            ((1,), (0,)),
        )
        for a, (row, rim) in rim_of.items()
    }
    side = 1 if flip else -1
    found = []
    for row in range(total):
        wide = slice(row * cols, (row + 1) * cols)
        parts = []
        for b in range(3):
            value = ref[b * mine : (b + 1) * mine, wide]
            if row in rim_row:
                value = value + rim_row[row][b * mine : (b + 1) * mine, :]
            parts.append(value)
        found.append(scale * (parts[1] + moved(parts[0], side) + moved(parts[2], -side)))
    return found


def hidden_kernel(total, scale, edge, fh, fl, pre_ref, hh, hl, slope_ref):
    cols = edge.shape[1]
    for row, pre in enumerate(
        row_sums(scale, fh, fl, pre_ref, rims(edge, 0, 2, total - 1), total, False)
    ):
        sig = jax.nn.sigmoid(pre)
        hidden = pre * sig
        slope_ref[:, row * cols : (row + 1) * cols] = sig * (1.0 + pre * (1.0 - sig))
        for b, value in enumerate((moved(hidden, -1), hidden, moved(hidden, 1))):
            put(hh, hl, b, row, value)


def either(wanted, scale, out, x_edge, c_edge, xh, xl, ch, cl, hh, hl, dh, dl, last):

    @pl.when(wanted == 0)
    def _():
        layer_grad(out, scale, dh, dl, xh, xl, rims(x_edge, 0, 2, last))

    @pl.when(wanted == 1)
    def _():
        layer_grad(out, scale, hh, hl, ch, cl, rims(c_edge, 2, 0, last))


def give_kernel(total, scale, *refs):
    x_edge, c_edge, xh, xl, ch, cl, hh, hl, slope_ref, gh, gl, back_ref = refs[:12]
    give_ref, dh, dl = refs[12:]
    cols = x_edge.shape[1]
    for row, dhidden in enumerate(
        row_sums(scale, gh, gl, back_ref, rims(c_edge, 2, 0, total - 1), total, True)
    ):
        dpre = dhidden * slope_ref[:, row * cols : (row + 1) * cols]
        for b, value in enumerate((moved(dpre, 1), dpre, moved(dpre, -1))):
            put(dh, dl, b, row, value)
    wanted = 1 - lax.axis_index("core")
    either(wanted, scale, give_ref, x_edge, c_edge, xh, xl, ch, cl, hh, hl, dh, dl, total - 1)


def keep_kernel(total, scale, *refs):
    x_edge, c_edge, xh, xl, ch, cl, hh, hl, dh, dl, keep_ref = refs
    wanted = lax.axis_index("core")
    either(wanted, scale, keep_ref, x_edge, c_edge, xh, xl, ch, cl, hh, hl, dh, dl, total - 1)


def gram_kernel(v_ref, out):
    count = v_ref.shape[0]
    col = lax.broadcasted_iota(jnp.int32, out.shape, 1)
    total = jnp.zeros(out.shape, F32)
    for i in range(count):
        for j in range(i, count):
            value = jnp.sum(v_ref[i] * v_ref[j], keepdims=True)
            total = jnp.where((col == i * count + j) | (col == j * count + i), value, total)
    out[...] = total


def merge_kernel(n_band, sums_ref, v_ref, f_ref, rate_ref, out):
    core = lax.axis_index("core")
    count = v_ref.shape[0]
    sums = sums_ref[...]
    lanes = sums.shape[1]
    device = lax.broadcasted_iota(jnp.int32, sums.shape, 0)
    same = ((device // n_band) % 2) == core
    flat = jnp.sum(jnp.where(same, sums, 0.0), 0, keepdims=True)
    row = lax.broadcasted_iota(jnp.int32, (count, lanes), 0)
    col = lax.broadcasted_iota(jnp.int32, (count, lanes), 1)
    gram = jnp.broadcast_to(flat, (count, lanes))
    wide = gram
    for i in range(1, count):
        gram = jnp.where(row == i, pltpu.roll(wide, lanes - i * count, 1), gram)
    gram = jnp.where(col < count, gram, 0.0)

    def swap(value, axis, step):
        size = value.shape[axis]
        index = row if axis == 0 else col
        return jnp.where(
            (index & step) != 0,
            pltpu.roll(value, step, axis),
            pltpu.roll(value, size - step, axis),
        )

    weight = jnp.ones((count, 1), F32)
    step = 1
    while step < count:
        own = jnp.where(row == col, gram, 0.0)
        cross = jnp.where((row ^ step) == col, gram, 0.0)
        down = 1.0 - jnp.sum(cross, 1, keepdims=True) / (
            2.0 * (jnp.sum(own, 1, keepdims=True) + 1e-06)
        )
        along = 1.0 - jnp.sum(cross, 0, keepdims=True) / (
            2.0 * (jnp.sum(own, 0, keepdims=True) + 1e-06)
        )
        weight = weight * down
        gram = gram * down * along
        gram = gram + swap(gram, 0, step)
        gram = gram + swap(gram, 1, step)
        step *= 2
    total = jnp.zeros(out.shape, F32)
    for i in range(count):
        total = total + weight[i : i + 1, :] * v_ref[i]
    out[...] = f_ref[...] - rate_ref[...] * total


def gather_kernel(*refs):
    parts, out = refs[:-1], refs[-1]
    pair = lax.axis_index("pair")
    size = parts[0].shape[0]
    for k, part in enumerate(parts):
        start = pl.multiple_of(lax.bitwise_xor(pair, k) * size, 8)
        out[pl.ds(start, size), :] = part[...]


def new_layer(n_pair, n_lo, layer, pieces, held, fresh):
    band = lax.axis_index("half") * n_lo + lax.axis_index("lo")
    size = pieces[0].shape[0] // n_pair
    chans = fresh.shape[1]
    mine = chans // n_lo
    for k, piece in enumerate(pieces):
        place = lax.bitwise_xor(band, k)
        half, lo = place // n_lo, place % n_lo
        for p in range(n_pair):
            to = pl.ds(pl.multiple_of((2 * p + half) * size, 8), size)
            held[lo, to, :] = piece[p * size : (p + 1) * size, :]
    for l in range(2):

        @pl.when(layer == l)
        def _():
            for t in range(9):
                at = pl.ds(t, chans, stride=9)
                value = held[:, t * mine : (t + 1) * mine, :].reshape(chans, chans)
                if l == 0:
                    value = value.T
                fresh[at, :] = value


def own_kernel(n_pair, n_lo, *refs):
    pieces, (fresh, held) = refs[:-2], refs[-2:]
    new_layer(n_pair, n_lo, lax.axis_index("core"), pieces, held, fresh)


def final_kernel(n_pair, n_lo, mine_ref, *refs):
    pieces, (out, held, fresh, sems) = refs[:-4], refs[-4:]
    core = lax.axis_index("core")
    first = pltpu.make_async_copy(mine_ref, out.at[0, core], sems.at[0])
    first.start()
    new_layer(n_pair, n_lo, 1 - core, pieces, held, fresh)
    second = pltpu.make_async_copy(fresh, out.at[0, 1 - core], sems.at[1])
    second.start()
    first.wait()
    second.wait()


def xor_route(count, k):
    return [(i, i ^ k) for i in range(count)]


def swapped(value, axis, k):
    return lax.ppermute(value, axis, xor_route(lax.axis_size(axis), k))


def routes():
    def at(core, half, lo):
        return (core * 2 + half) * 2 + lo

    every = [(core, half, lo) for core in range(2) for half in range(2) for lo in range(2)]
    near = [(at(c, h, l), at(h, c, 1 - l if c == h else l)) for c, h, l in every]
    far = [(at(c, h, l), at(h, c, 1 - l)) for c, h, l in every if c != h]
    onward = [(at(c, h, l), at(c, h, 1 - l)) for c, h, l in every if c != h]
    return near, far, onward


def sent(value, route):
    return lax.ppermute(value, ("core", "half", "lo"), route)


def fast(images, cotangent, filters, rates):
    _, chans, rows, cols = images.shape
    n_pair, n_lo = lax.axis_size("pair"), lax.axis_size("lo")
    n_image, n_band = 2 * n_pair, 2 * n_lo
    kdim = filters.shape[1]
    mine = chans // n_lo
    total = n_lo * rows
    slot = 9 * mine // n_image
    flat = (chans * rows, cols)
    bf = lambda *shape: jax.ShapeDtypeStruct(shape, BF16)
    tall, thin, wide = 3 * chans, 3 * mine, total * cols
    near, far, onward = routes()
    c_near = sent(cotangent, near)
    x_near = sent(images, near)
    x_far = sent(images, far)
    c_far = sent(c_near, onward)
    xs = [v.reshape(flat) for v in (images, x_near, x_far)]
    cs = [v.reshape(flat) for v in (cotangent, c_near, c_far)]
    vmem, smem = (pl.BlockSpec(memory_space=m) for m in (pltpu.VMEM, pltpu.SMEM))
    params = pltpu.CompilerParams(vmem_limit_bytes=40 * 2**20)
    like = lambda *shape: jax.ShapeDtypeStruct(shape, F32)
    fh, fl, gh, gl, tapped, rate = pl.pallas_call(
        filter_kernel,
        out_shape=[bf(thin, tall)] * 4 + [like(slot, chans), like(1, chans)],
        in_specs=[smem, vmem],
        out_specs=[vmem] * 6,
        scratch_shapes=[
            pltpu.VMEM((2, 9, chans, chans), F32),
            pltpu.VMEM((2, 9 * mine, chans), F32),
        ],
        compiler_params=params,
    )(rates, filters)
    (edge,) = call(edge_kernel, [(chans, cols)])(*xs)
    x_edge = swapped(edge, "core", 1)
    raw = [pltpu.VMEM((total, chans, cols), F32)]
    work = 6 * thin * tall * wide
    outs = [bf(tall, wide)] * 2 + [(thin, wide)]
    xh, xl, pre = call(functools.partial(rows_kernel, False), outs, raw, flops=work)(*xs, fh, fl)
    scale = kdim ** (-0.5)
    hh, hl, slope = call(
        functools.partial(hidden_kernel, total, scale), [bf(thin, wide)] * 2 + [(mine, wide)]
    )(x_edge, fh, fl, pre)
    (edge,) = call(edge_kernel, [(chans, cols)])(*cs)
    c_edge = swapped(edge, "core", 1)
    ch, cl, back = call(functools.partial(rows_kernel, True), outs, raw, flops=work)(*cs, gh, gl)
    rows_of = (x_edge, c_edge, xh, xl, ch, cl, hh, hl)
    part = (9 * mine, chans)
    give, dh, dl = call(
        functools.partial(give_kernel, total, scale), [part] + [bf(thin, wide)] * 2, flops=2 * work
    )(*rows_of, slope, gh, gl, back)
    given = swapped(give, "core", 1)
    (keep,) = call(
        functools.partial(keep_kernel, total, scale), [part], flops=work
    )(*rows_of, dh, dl)
    whole = keep + given
    slices = lax.all_to_all(
        whole.reshape(n_image, slot, chans), ("pair", "half"), 0, 0, tiled=True
    )
    (gram,) = call(gram_kernel, [(1, 128)])(slices)
    sums = jnp.broadcast_to(gram, (n_image * n_band, gram.shape[1]))
    sums = lax.all_to_all(sums, AXES, 0, 0, tiled=True)
    (merged,) = call(functools.partial(merge_kernel, n_band), [(slot, chans)])(
        sums, slices, tapped, rate
    )
    pieces = [merged] + [swapped(merged, "pair", k) for k in range(1, n_pair)]
    (block,) = call(gather_kernel, [(n_pair * slot, chans)])(*pieces)
    own = [block] + [swapped(block, ("half", "lo"), k) for k in range(1, n_band)]
    others = [swapped(piece, "core", 1) for piece in own]
    layer = (kdim, chans)
    held = pltpu.VMEM((n_lo,) + part, F32)
    fresh = pl.pallas_call(
        functools.partial(own_kernel, n_pair, n_lo),
        out_shape=jax.ShapeDtypeStruct(layer, F32),
        in_specs=[vmem] * n_band,
        out_specs=vmem,
        scratch_shapes=[held],
        compiler_params=params,
    )(*own)
    return pl.pallas_call(
        functools.partial(final_kernel, n_pair, n_lo),
        out_shape=jax.ShapeDtypeStruct((1,) + filters.shape, F32),
        in_specs=[vmem] * (1 + n_band),
        out_specs=pl.BlockSpec(memory_space=pl.ANY),
        scratch_shapes=[held, pltpu.VMEM(layer, F32), pltpu.SemaphoreType.DMA((2,))],
        compiler_params=params,
    )(fresh, *others)


def with_rims(field):
    count = lax.axis_size("band")
    forward = [(i, i + 1) for i in range(count - 1)]
    backward = [(target, source) for source, target in forward]
    low = lax.ppermute(field[:, -1:], "band", forward)
    high = lax.ppermute(field[:, :1], "band", backward)
    extended = jnp.concatenate([low, field, high], axis=1)
    return jnp.pad(extended, ((0, 0), (0, 0), (1, 1)))


def taps(padded, rows, cols, flip=False):
    chans = padded.shape[0]
    at = (2, 1, 0) if flip else (0, 1, 2)
    pieces = [padded[:, dr : dr + rows, dc : dc + cols] for dr in at for dc in at]
    return jnp.stack(pieces, axis=1).reshape(chans, 9, rows * cols)


def plain(images, cotangent, filters, rates):
    feats, cot = images[0], cotangent[0]
    chans, rows, cols = feats.shape
    scale = (9 * chans) ** (-0.5)
    patch_one = taps(with_rims(feats), rows, cols).reshape(9 * chans, rows * cols)
    pre = scale * jnp.einsum("kc,kp->cp", filters[0], patch_one, precision=HIGH)
    hidden = jax.nn.silu(pre).reshape(chans, rows, cols)
    patch_two = taps(with_rims(hidden), rows, cols).reshape(9 * chans, rows * cols)
    back = taps(with_rims(cot), rows, cols, flip=True)
    flat_cot = cot.reshape(chans, rows * cols)
    grad_two = scale * jnp.einsum("kp,cp->kc", patch_two, flat_cot, precision=HIGH)
    weight_two = filters[1].reshape(chans, 9, chans)
    dhidden = scale * jnp.einsum("itc,ctp->ip", weight_two, back, precision=HIGH)
    sig = jax.nn.sigmoid(pre)
    dpre = dhidden * sig * (1.0 + pre * (1.0 - sig))
    grad_one = scale * jnp.einsum("kp,cp->kc", patch_one, dpre, precision=HIGH)
    block = lax.psum_scatter(
        jnp.stack([grad_one, grad_two]), "band", scatter_dimension=1, tiled=True
    )
    count = lax.axis_size("image")
    for level in range(count.bit_length() - 1):
        other = lax.ppermute(block, "image", xor_route(count, 1 << level))
        inner, own_sq, other_sq = lax.psum(
            tuple(jnp.sum(v, axis=(1, 2)) for v in (block * other, block * block, other * other)),
            "band",
        )
        low = (1.0 - inner / (2.0 * (own_sq + 1e-06)))[:, None, None]
        high = (1.0 - inner / (2.0 * (other_sq + 1e-06)))[:, None, None]
        block = low * block + high * other
    height = block.shape[1]
    mine = lax.dynamic_slice_in_dim(filters, lax.axis_index("band") * height, height, 1)
    fresh = (mine - rates[:, None, None] * block)[None]
    return lax.all_gather(fresh, "band", axis=2, tiled=True)


def power_of_two(n):
    return n & (n - 1) == 0


def solution(mesh):
    n_image, n_band = mesh.shape["image"], mesh.shape["band"]

    def step(images, cotangent, filters, rates):
        chans = images.shape[1]
        if (
            4 <= n_image
            and n_image**2 <= 128
            and n_band == 4
            and power_of_two(n_image)
            and (9 * chans) % (n_band // 2 * n_image * 8) == 0
        ):
            shape = (n_image // 2, 2, 2, n_band // 2)
            split = jax.sharding.Mesh(mesh.devices.reshape(shape), AXES)
            image, band = ("pair", "core"), ("half", "lo")

            def body(*args):
                return fast(*args)

        else:
            split, image, band, body = mesh, "image", "band", plain
        whole = jax.shard_map(
            body,
            mesh=split,
            in_specs=(P(image, None, band, None), P(image, None, band, None), P(), P()),
            out_specs=P(image, None, None, None),
            check_vma=False,
        )
        return whole(images, cotangent, filters, rates)

    return step
```
